32 devices in a mesh: pipe: 4 (over y, x), dp: 8 (over z, core).
Axes of the slice: x: 2, y: 2, z: 4, core: 2. Of those that a mesh axis runs over, the one named last changes fastest.
Arguments:
- inputs: bfloat16 [8, 4, 32, 8192], P('dp'), may hold values from -48 to 48
- segments: int32 [8, 4, 32], P('dp'), may hold values from 0 to 3, never falling along the last dimension, each value on 1 to 16 neighbouring positions
- cotangent: bfloat16 [8, 4, 32, 8192], P('dp'), may hold values from -6 to 6
- w_query: bfloat16 [4, 8192, 128], P('pipe', 'dp'), may hold values from -3 to 3
- w_key: bfloat16 [4, 8192, 128], P('pipe', 'dp'), may hold values from -3 to 3
- w_value: bfloat16 [4, 8192, 128], P('pipe', 'dp'), may hold values from -0.0625 to 0.0625
- w_out: bfloat16 [4, 8192, 128], P('pipe', 'dp'), may hold values from -0.5 to 0.5
Outputs:
- input_grads: bfloat16 [4, 8, 4, 32, 8192], P('pipe', 'dp')
- grad_query: float32 [4, 8192, 128], P('pipe', 'dp')
- grad_key: float32 [4, 8192, 128], P('pipe', 'dp')
- grad_value: float32 [4, 8192, 128], P('pipe', 'dp')
- grad_out: float32 [4, 8192, 128], P('pipe', 'dp')
The draws below stay inside these ranges and needn't reach their ends.
Inputs may be any that keep to these rules, and one draw needn't show every extreme that they name: `segments`: along each micro-batch the numbers never fall; a document has 1 to 16 tokens, and one has exactly 16.
All inputs are finite; a program needn't handle non-finite values.
Results may differ from the reference program's by a relative error of at most 0.025.
Values may be sent and summed in bfloat16 or wider, within the bound.
No kernel may reach another device: no remote copies, remote signals or barrier semaphores. Data moves between devices by JAX's collectives and lax.ppermute only.
A program may use at most 192 MiB of HBM per device.

```python
import math
import jax
import jax.numpy as jnp
import numpy as np
from jax import lax

D = 8192
HD = 128
MB = 4
SEQ = 32
SECTIONS = 4
MOST = 16
N_DP = 8


def projection_draw(key, salt):
    drawn = jax.random.truncated_normal(jax.random.fold_in(key, salt), -4.0, 4.0, (SECTIONS, D, HD), jnp.float32) / math.sqrt(D)
    return drawn.astype(jnp.bfloat16)


def draw_w_query(key, part):
    return projection_draw(key, 11)


def draw_w_key(key, part):
    return projection_draw(key, 12)


def draw_inputs(key, part):
    shape = (N_DP, MB, SEQ, D)
    pairing = jax.random.permutation(jax.random.fold_in(key, 21), N_DP)
    column_block = jnp.arange(D) // (D // N_DP)
    paired = (pairing[:, None] == column_block[None, :]).astype(jnp.float32)
    boost = (1.0 + 3.0 * paired)[:, None, None, :]
    base = jax.random.truncated_normal(jax.random.fold_in(key, 22), -6.0, 6.0, shape, jnp.float32) * boost
    return base.astype(jnp.bfloat16)


def steps_of(own_key, shape, cuts, low, high):
    loudness, own = 1.0, jax.random.fold_in(own_key, 6)
    for axis_at, blocks in cuts:
        heights = jnp.exp(jax.random.uniform(jax.random.fold_in(own, axis_at), (blocks,), jnp.float32, low / len(cuts), high / len(cuts)))
        loudness = loudness * jnp.repeat(heights, shape[axis_at] // blocks).reshape([-1 if axis == axis_at else 1 for axis in range(len(shape))])
    return loudness


def split_up(number_of, total, bound, lean):
    weights = [(1 << 20) // math.isqrt(standing ** lean) + 1 for standing in range(2, number_of + 1)]
    surplus, given = total - bound - (number_of - 1), [1] * (number_of - 1)
    while surplus > 0:
        free = [i for i in range(number_of - 1) if given[i] < bound]
        pool, remaining = sum([weights[i] for i in free]), surplus
        for i in free:
            addition = min(bound - given[i], max(1, remaining * weights[i] // pool), surplus)
            given[i] = given[i] + addition
            surplus = surplus - addition
    return np.array([bound] + given)


def uneven(rng, number_of, total, most, slope):
    if number_of == 2:
        one = jax.random.randint(rng, (), max(1, total - most), min(most, total - 1) + 1)
        return jnp.stack([one, total - one])
    sizes = jnp.asarray(split_up(number_of, total, most, slope), jnp.int32)
    couples = (number_of - 1) // 2
    giver, receiver = sizes[1:1 + 2 * couples:2], sizes[2:2 + 2 * couples:2]
    slack = jnp.minimum(giver - 1, most - receiver)
    moved = jax.random.randint(jax.random.fold_in(rng, 1), (couples,), 0, 1 << 20) % (slack + 1)
    sizes = sizes.at[1:1 + 2 * couples:2].set(giver - moved).at[2:2 + 2 * couples:2].set(receiver + moved)
    return sizes[jax.random.permutation(jax.random.fold_in(rng, 2), number_of)]


def gaussian(own_key, dims, scale, limit, split=(), dtype=jnp.bfloat16):
    result = scale * jax.random.normal(own_key, dims, jnp.float32)
    if split:
        result = result * steps_of(own_key, dims, split, -0.22, 0.18)
    return jnp.clip(result, -limit, limit).astype(dtype)


def setup_inputs(seed: int = 0) -> dict:
    seeds = jax.random.split(jax.random.key(seed), 8)
    inputs = draw_inputs(jax.random.fold_in(seeds[7], 71), 0)
    segments = jax.vmap(lambda own: jnp.searchsorted(jnp.cumsum(uneven(own, 4, SEQ, MOST, 0)), jnp.arange(SEQ), side="right"))(jax.random.split(seeds[1], N_DP * MB)).reshape((N_DP, MB, SEQ)).astype(jnp.int32)
    cotangent = gaussian(seeds[2], (N_DP, MB, SEQ, D), 1.0, 6.0, ((0, 8),))
    w_query = draw_w_query(jax.random.fold_in(seeds[7], 71), 0)
    w_key = draw_w_key(jax.random.fold_in(seeds[7], 71), 0)
    w_value = gaussian(seeds[5], (SECTIONS, D, HD), D ** -0.5, 0.0625, ((0, 4), (1, 8)))
    w_out = gaussian(seeds[6], (SECTIONS, D, HD), HD ** -0.5, 0.5, ((0, 4), (1, 8)))
    return {"inputs": inputs, "segments": segments, "cotangent": cotangent, "w_query": w_query, "w_key": w_key, "w_value": w_value, "w_out": w_out}


def section(hidden, doc_ids, w_query, w_key, w_value, w_out):
    widen = hidden.astype(jnp.float32)
    normed = (widen * lax.rsqrt(lax.optimization_barrier(jnp.mean(widen * widen, axis=-1, keepdims=True)) + 1e-05)).astype(jnp.bfloat16)
    query = jnp.dot(normed, w_query, preferred_element_type=jnp.float32).astype(jnp.bfloat16)
    keys = jnp.dot(normed, w_key, preferred_element_type=jnp.float32).astype(jnp.bfloat16)
    values = jnp.dot(normed, w_value, preferred_element_type=jnp.float32).astype(jnp.bfloat16)
    scores = jnp.dot(query, keys.T, preferred_element_type=jnp.float32) * w_query.shape[1] ** (-0.5)
    places = jnp.arange(hidden.shape[0])
    allowed = (places[:, None] >= places[None, :]) & (doc_ids[:, None] == doc_ids[None, :])
    scores = jnp.where(allowed, scores, -1e+30)
    highest = lax.optimization_barrier(jnp.max(scores, axis=-1, keepdims=True))
    exponent = jnp.where(allowed, jnp.exp(scores - highest), 0.0)
    attend = (exponent / lax.optimization_barrier(jnp.sum(exponent, axis=-1, keepdims=True))).astype(jnp.bfloat16)
    mixed = jnp.dot(attend, values, preferred_element_type=jnp.float32).astype(jnp.bfloat16)
    update = jnp.dot(mixed, w_out.T, preferred_element_type=jnp.float32)
    return (widen + update).astype(jnp.bfloat16)

def reference(inputs, segments, cotangent, w_query, w_key, w_value, w_out):
    weights = (w_query, w_key, w_value, w_out)

    def one_sequence(start, doc_ids, final_cot):

        def forward(hidden, layer):
            return (section(hidden, doc_ids, *layer), hidden)
        _, saved = lax.scan(forward, start, weights)

        def backward(carried, item):
            saved_h, layer = item
            _, pull = jax.vjp(lambda hid, wa, wb, wc, wd: section(hid, doc_ids, wa, wb, wc, wd), saved_h, *layer)
            outs = pull(carried)
            return (outs[0], outs)
        _, results = lax.scan(backward, final_cot, (saved, weights), reverse=True)
        return results

    def replica(totals, item):
        start, doc_ids, final_cot = item
        results = jax.vmap(one_sequence)(start, doc_ids, final_cot)
        partials = []
        for grad in results[1:]:
            summed = lax.optimization_barrier(jnp.sum(grad.astype(jnp.float32), axis=0)).astype(jnp.bfloat16)
            summed = lax.optimization_barrier(summed)
            partials.append(summed.astype(jnp.float32))
        new_totals = tuple((total + part for total, part in zip(totals, partials)))
        return (new_totals, results[0])
    zeros = tuple((jnp.zeros(w_query.shape, jnp.float32) for _ in range(4)))
    totals, input_all = lax.scan(replica, zeros, (inputs, segments, cotangent))
    input_grads = jnp.transpose(input_all, (2, 0, 1, 3, 4))
    return (input_grads, totals[0], totals[1], totals[2], totals[3])
```

```python
import functools

import jax
import jax.numpy as jnp
from jax import lax
from jax.experimental import pallas as pl
from jax.experimental.pallas import tpu as pltpu
from jax.sharding import PartitionSpec as P

BF = jnp.bfloat16
F32 = jnp.float32
NN = (((1,), (0,)), ((), ()))
NT = (((1,), (1,)), ((), ()))
TN = (((0,), (0,)), ((), ()))
VMEM_BYTES = 56 * 2**20
CORES = 2


def dot(a, b, dims=NN):
    return lax.dot_general(a, b, dims, preferred_element_type=F32)


def hop(block, axis, step):
    return lax.ppermute(block, axis, [(i, i ^ step) for i in range(lax.axis_size(axis))])


def place():
    b = lax.axis_index("dp")
    return lax.axis_index("pipe"), b // CORES, b % CORES


def vmem(count):
    return [pl.BlockSpec(memory_space=pltpu.VMEM)] * count


def anywhere(count):
    return [pl.BlockSpec(memory_space=pl.ANY)] * count


def pack(features, cots, chips):
    _, total, seq, width = features.shape
    group = total // lax.axis_size("pipe")
    eighth = width // (chips * CORES)

    def kernel(x_ref, g_ref, *rest):
        outs, sems = rest[:chips], rest[chips]
        p, z, c = place()
        copies = []
        for k in range(chips):
            for h in range(CORES):
                start = pl.multiple_of(((z ^ k) * CORES + (c ^ h)) * eighth, eighth)
                for a, ref in enumerate((x_ref, g_ref)):
                    copies.append(
                        pltpu.make_async_copy(
                            ref.at[0, pl.ds(p * group, group), :, pl.ds(start, eighth)],
                            outs[k].at[a, :, :, pl.ds(h * eighth, eighth)],
                            sems.at[len(copies)],
                        )
                    )
        for copy in copies:
            copy.start()
        for copy in copies:
            copy.wait()

    piece = jax.ShapeDtypeStruct((2, group, seq, CORES * eighth), BF)
    outs = pl.pallas_call(
        kernel,
        name="pack",
        out_shape=[piece] * chips,
        in_specs=anywhere(2),
        out_specs=vmem(chips),
        scratch_shapes=[pltpu.SemaphoreType.DMA((chips * CORES * 2,))],
    )(features, cots)
    return [out.reshape(2, group * seq, CORES * eighth) for out in outs]


def unpack(pieces, chips, width):
    rows, eighth = pieces[0].shape

    def kernel(*refs):
        ins, out, sems = refs[:-2], refs[-2], refs[-1]
        _, z, c = place()
        copies = []
        for k in range(chips):
            for h in range(CORES):
                start = pl.multiple_of(((z ^ k) * CORES + (c ^ h)) * eighth, eighth)
                copies.append(
                    pltpu.make_async_copy(
                        ins[k * CORES + h], out.at[:, pl.ds(start, eighth)], sems.at[len(copies)]
                    )
                )
        for copy in copies:
            copy.start()
        for copy in copies:
            copy.wait()

    return pl.pallas_call(
        kernel,
        name="unpack",
        out_shape=jax.ShapeDtypeStruct((rows, width), BF),
        in_specs=vmem(len(pieces)),
        out_specs=pl.BlockSpec(memory_space=pl.ANY),
        scratch_shapes=[pltpu.SemaphoreType.DMA((len(pieces),))],
    )(*pieces)


def project(tokens, own, other, head):
    chips, sections = len(tokens), len(own)
    rows = tokens[0].shape[1]
    half = own[0].shape[0]

    def kernel(*refs):
        tok = refs[:chips]
        ws = refs[chips : chips + sections]
        vs = refs[chips + sections : chips + 2 * sections]
        outs = refs[chips + 2 * sections : 2 * chips + 2 * sections]
        gram = refs[-1]
        p, _, c = place()
        h = jnp.concatenate([t[0] for t in tok], axis=0)
        g = jnp.concatenate([t[1] for t in tok], axis=0)
        for j in range(sections):
            a = dot(h[:, :half], ws[j][...]) + dot(h[:, half:], vs[j][...])
            b = dot(g[:, :half], ws[j][:, 3 * head :]) + dot(g[:, half:], vs[j][:, 3 * head :])
            for k in range(chips):
                outs[k][j, :, : 4 * head] = a[k * rows : (k + 1) * rows]
                outs[k][j, :, 4 * head :] = b[k * rows : (k + 1) * rows]

        def put(j, low, high, block):
            cols = slice(block * head, (block + 1) * head)
            gram[j] = sum(
                dot(w[low][:, 3 * head :], w[high][:, cols], TN) for w in (ws, vs)
            )

        put(0, 0, 0, 3)
        for j in range(1, sections):
            below = p < (p ^ j)
            for core in range(CORES):
                pl.when(below & (c == core))(functools.partial(put, j, 0, j, core))
                pl.when(jnp.logical_not(below) & (c == core))(
                    functools.partial(put, j, j, 0, CORES + core)
                )

    outs = pl.pallas_call(
        kernel,
        name="project",
        out_shape=[jax.ShapeDtypeStruct((sections, rows, 5 * head), F32)] * chips
        + [jax.ShapeDtypeStruct((sections, head, head), F32)],
        in_specs=vmem(chips + 2 * sections),
        out_specs=vmem(chips + 1),
        compiler_params=pltpu.CompilerParams(vmem_limit_bytes=VMEM_BYTES),
    )(*tokens, *own, *other)
    return outs[:chips], outs[chips]


def chain(partials, squares, docs, grams, head, width, seq):
    sections = len(grams)
    parts = len(partials)
    rows = squares.shape[0]
    lanes = sections * 4 * head

    def kernel(*refs):
        a_refs = refs[:parts]
        sq_ref, dr_ref, dc_ref = refs[parts : parts + 3]
        g_refs = refs[parts + 3 : parts + 3 + sections * CORES]
        out, a_all, hi, lo = refs[parts + 3 + sections * CORES :]
        p, _, c = place()
        for j in range(sections):
            total = a_refs[0][j]
            for ref in a_refs[1:]:
                total = total + ref[j]
            a_all[p ^ j] = total
        for i in range(sections):
            for h in range(CORES):
                for j in range(sections):
                    if j == 0 and h > 0:
                        continue
                    block = g_refs[i * CORES + h][j]
                    coarse = block.astype(BF)
                    fine = (block - coarse.astype(F32)).astype(BF)
                    one, two = p ^ i, p ^ i ^ j
                    low, high = jnp.minimum(one, two), jnp.maximum(one, two)
                    if j == 0:
                        kind = 3
                    else:
                        kind = jnp.where(one < two, 0, CORES) + (c ^ h)
                    hi[low, high, kind] = coarse
                    lo[low, high, kind] = fine

        def times(m, low, high, kind, dims=NN):
            return dot(m, hi[low, high, kind], dims) + dot(m, lo[low, high, kind], dims)

        places_r = lax.broadcasted_iota(jnp.int32, (rows, rows), 0)
        places_c = lax.broadcasted_iota(jnp.int32, (rows, rows), 1)
        allowed = (places_r >= places_c) & (dr_ref[...] == dc_ref[...])
        if rows > seq:
            allowed = allowed & (places_r // seq == places_c // seq)
        scale = head ** (-0.5)

        x = [[a_all[s, :, i * head : (i + 1) * head] for i in range(3)] for s in range(sections)]
        ho = [a_all[s, :, 3 * head : 4 * head] for s in range(sections)]
        bo = [a_all[s, :, 4 * head :] for s in range(sections)]
        norm = sq_ref[...]
        saved = []
        for s in range(sections):
            inv = lax.rsqrt(jnp.maximum(norm, 0.0) / width + 1e-05)
            q, k, v = ((part * inv).astype(BF) for part in x[s])
            scores = jnp.where(allowed, dot(q, k, NT) * scale, -1e30)
            highest = jnp.max(scores, axis=-1, keepdims=True)
            exponent = jnp.where(allowed, jnp.exp(scores - highest), 0.0)
            soft = exponent / jnp.sum(exponent, axis=-1, keepdims=True)
            attend = soft.astype(BF)
            mixed = dot(attend, v).astype(BF)
            saved.append((inv, q, k, v, soft, attend, mixed, list(ho)))
            if s < sections - 1:
                before = ho[s]
                for t in range(s + 1, sections):
                    x[t] = [x[t][i] + times(mixed, s, t, i) for i in range(3)]
                for t in range(sections - 1):
                    if t >= s:
                        ho[t] = ho[t] + times(mixed, s, t, 3)
                    else:
                        ho[t] = ho[t] + times(mixed, t, s, 3, NT)
                wide = mixed.astype(F32)
                norm = norm + jnp.sum(wide * (before + ho[s]), axis=-1, keepdims=True)

        lane = lax.broadcasted_iota(jnp.int32, (rows, head), 1)
        scalars = jnp.zeros((rows, head), F32)
        for s in reversed(range(sections)):
            inv, q, k, v, soft, attend, mixed, along = saved[s]
            d_mixed = bo[s].astype(BF)
            d_attend = dot(d_mixed, v, NT).astype(BF).astype(F32)
            d_values = dot(attend, d_mixed, TN)
            inner = jnp.sum(soft * d_attend, axis=-1, keepdims=True)
            d_scores = (soft * (d_attend - inner) * scale).astype(BF)
            d_query = dot(d_scores, k)
            d_keys = dot(d_scores, q, TN)
            y = [(part * inv).astype(BF) for part in (d_query, d_keys, d_values)]
            inner = sum(y[i].astype(F32) * x[s][i] for i in range(3))
            coef = inv * inv * jnp.sum(inner, axis=-1, keepdims=True) / width
            for t in range(s):
                add = sum(times(y[i], t, s, i, NT) for i in range(3))
                bo[t] = bo[t] + add - coef * along[t]
            at = s * 4 * head
            for i in range(3):
                out[:, at + i * head : at + (i + 1) * head] = y[i]
            out[:, at + 3 * head : at + 4 * head] = mixed
            coarse = coef.astype(BF).astype(F32)
            scalars = jnp.where(lane == 2 * s, coarse, scalars)
            scalars = jnp.where(lane == 2 * s + 1, coef - coarse, scalars)
        out[:, lanes:] = scalars.astype(BF)

    return pl.pallas_call(
        kernel,
        name="chain",
        out_shape=jax.ShapeDtypeStruct((rows, lanes + head), BF),
        in_specs=vmem(parts + 3 + sections * CORES),
        out_specs=pl.BlockSpec(memory_space=pltpu.VMEM),
        scratch_shapes=[
            pltpu.VMEM((sections, rows, 5 * head), F32),
            pltpu.VMEM((sections, sections, 4, head, head), BF),
            pltpu.VMEM((sections, sections, 4, head, head), BF),
        ],
        compiler_params=pltpu.CompilerParams(vmem_limit_bytes=VMEM_BYTES),
    )(*partials, squares, docs[:, None], docs[None, :], *[g for pair in grams for g in pair])


def factors(p, j, sections, head, section_of, scalars):
    s = p ^ j
    both = section_of(s)
    side = lax.broadcasted_iota(jnp.int32, scalars.shape, 1) // 2
    after = jnp.where((side > jnp.maximum(p, s)) & (side < sections), scalars, 0.0)
    share = jnp.where(s >= p, jnp.sum(after, axis=-1, keepdims=True), 0.0)
    y = both[:, : 3 * head]
    m = both[:, 3 * head :]
    into_g = (
        jnp.where(s > p, y, jnp.zeros_like(y)),
        (-share * m.astype(F32)).astype(BF),
    )
    into_h = jnp.where(s < p, m, jnp.zeros_like(m))
    return into_g, into_h, share


def rebuild(tokens, coefs, weights, column, columns, head):
    sections, chips = len(weights), len(tokens[0])
    rows, lanes = coefs[0][0].shape
    half = weights[0].shape[0]
    groups = len(tokens)
    count = groups * chips * rows
    block = min(256, half)
    steps = half // block
    flat_t = [t for line in tokens for t in line]
    flat_c = [t for line in coefs for t in line]

    def kernel(*refs):
        n = groups * chips
        t_refs, c_refs = refs[:n], refs[n : 2 * n]
        w_refs = refs[2 * n : 2 * n + sections]
        outs = refs[2 * n + sections : 2 * n + sections + chips]
        grads, left_g, left_h, own, edge = refs[2 * n + sections + chips :]
        p, _, _ = place()

        @pl.when(pl.program_id(0) == 0)
        def _():
            for i in range(n):
                at = pl.ds(i * rows, rows)
                scalars = c_refs[i][:, lanes - head :].astype(F32)
                ref = c_refs[i]

                def section_of(s, ref=ref):
                    return ref[:, pl.ds(pl.multiple_of(s * 4 * head, 4 * head), 4 * head)]

                for j in range(sections):
                    (g_y, g_m), into_h, share = factors(p, j, sections, head, section_of, scalars)
                    left_g[j, at, : 3 * head] = g_y
                    left_g[j, at, 3 * head :] = g_m
                    if j > 0:
                        left_h[j - 1, at, :] = into_h
                    else:
                        own[at, :] = section_of(p)
                        side = lax.broadcasted_iota(jnp.int32, scalars.shape, 1) // 2
                        here = jnp.where(side == p, scalars, 0.0)
                        here = jnp.sum(here, axis=-1, keepdims=True)
                        edge[0, at, :] = jnp.broadcast_to(share, (rows, head))
                        edge[1, at, :] = jnp.broadcast_to(here, (rows, head))

        h = jnp.concatenate([t[0] for t in t_refs], axis=0).astype(F32)
        g = jnp.concatenate([t[1] for t in t_refs], axis=0).astype(F32)
        for j in range(1, sections):
            h = h + dot(left_h[j - 1], w_refs[j][:, 3 * head :], NT)
        for j in range(sections):
            g = g + dot(left_g[j], w_refs[j][...], NT)
        g = g - edge[0][:, :1] * h
        y, m = own[:, : 3 * head], own[:, 3 * head :]
        grads[:, : 3 * head] = dot(h.astype(BF), y, TN)
        grads[:, 3 * head :] = dot(g.astype(BF), m, TN)
        result = (g + dot(y, w_refs[0][:, : 3 * head], NT) - edge[1][:, :1] * h).astype(BF)
        for j in range(groups):
            for k in range(chips):
                at = (j * chips + k) * rows
                outs[k][p ^ j] = result[at : at + rows]

    held = columns // block
    outs = pl.pallas_call(
        kernel,
        name="rebuild",
        grid=(steps,),
        out_shape=[jax.ShapeDtypeStruct((groups, rows, half), BF)] * chips
        + [jax.ShapeDtypeStruct((half, 4 * head), F32)],
        in_specs=[pl.BlockSpec((2, rows, block), lambda i: (0, 0, i + column // block))]
        * len(flat_t)
        + vmem(len(flat_c))
        + [pl.BlockSpec((block, 4 * head), lambda i: (i, 0))] * sections,
        out_specs=[pl.BlockSpec((groups, rows, block), lambda i: (0, 0, i))] * chips
        + [pl.BlockSpec((block, 4 * head), lambda i: (i, 0))],
        scratch_shapes=[
            pltpu.VMEM((sections, count, 4 * head), BF),
            pltpu.VMEM((sections - 1, count, head), BF),
            pltpu.VMEM((count, 4 * head), BF),
            pltpu.VMEM((2, count, head), F32),
        ],
        compiler_params=pltpu.CompilerParams(vmem_limit_bytes=VMEM_BYTES),
    )(*flat_t, *flat_c, *weights)
    return outs[:chips], outs[chips]


def rebuild_wide(tokens, coefs, weights, column, columns, head):
    sections, chips = len(weights), len(tokens[0])
    rows, lanes = coefs[0][0].shape
    half = weights[0].shape[0]
    p, _, _ = place()
    grads = jnp.zeros((half, 4 * head), F32)
    results = []
    for group, line in zip(tokens, coefs):
        both = jnp.concatenate([t[:, :, column : column + half] for t in group], axis=1)
        both, coef, grads = lax.optimization_barrier((both, jnp.concatenate(line, axis=0), grads))
        scalars = coef[:, lanes - head :].astype(F32)

        def section_of(s, coef=coef):
            return lax.dynamic_slice_in_dim(coef, s * 4 * head, 4 * head, axis=1)

        h, g = both[0].astype(F32), both[1].astype(F32)
        for j in range(sections):
            (g_y, g_m), into_h, share = factors(p, j, sections, head, section_of, scalars)
            h = h + dot(into_h, weights[j][:, 3 * head :], NT)
            g = g + dot(g_y, weights[j][:, : 3 * head], NT)
            g = g + dot(g_m, weights[j][:, 3 * head :], NT)
            if j == 0:
                ahead = share
        g = g - ahead * h
        own = section_of(p)
        y, m = own[:, : 3 * head], own[:, 3 * head :]
        side = lax.broadcasted_iota(jnp.int32, scalars.shape, 1) // 2
        here = jnp.sum(jnp.where(side == p, scalars, 0.0), axis=-1, keepdims=True)
        grads = grads + jnp.concatenate(
            [dot(h.astype(BF), y, TN), dot(g.astype(BF), m, TN)], axis=1
        )
        result = (g + dot(y, weights[0][:, : 3 * head], NT) - here * h).astype(BF)
        results.append(result.reshape(chips, rows, half))
    result = jnp.take(jnp.stack(results), jnp.arange(len(tokens)) ^ p, axis=0)
    return [result[:, k] for k in range(chips)], grads


def shards(inputs, segments, cotangent, w_query, w_key, w_value, w_out):
    sections = lax.axis_size("pipe")
    chips = lax.axis_size("dp") // CORES
    head = w_query.shape[2]
    _, batches, seq, width = inputs.shape
    section_id, _, _ = place()
    short = -batches % sections
    if short:
        fill = ((0, 0), (0, short), (0, 0), (0, 0))
        inputs, cotangent = jnp.pad(inputs, fill), jnp.pad(cotangent, fill)
        segments = jnp.pad(segments, fill[:3])
    group = inputs.shape[1] // sections
    rows = group * seq

    pieces = pack(inputs, cotangent, chips)
    mine = jnp.concatenate([w_query[0], w_key[0], w_value[0], w_out[0]], axis=1)
    pieces, mine = lax.optimization_barrier((pieces, mine))
    tokens = [pieces[0]] + [hop(pieces[k], "dp", k * CORES) for k in range(1, chips)]
    own = [mine] + [hop(mine, "pipe", j) for j in range(1, sections)]
    other = [hop(w, "dp", 1) for w in own]
    start = lax.dynamic_slice_in_dim(inputs[0], section_id * group, group, 0)
    start = start.reshape(rows, width).astype(F32)
    squares = jnp.sum(start * start, axis=-1, keepdims=True)
    docs = lax.dynamic_slice_in_dim(segments[0], section_id * group, group, 0).reshape(rows)

    partials, gram = project(tokens, own, other, head)
    partials = [partials[0]] + [hop(partials[k], "dp", k * CORES) for k in range(1, chips)]
    gram = sum([hop(gram, "dp", k * CORES) for k in range(1, chips)], gram)
    near = [gram] + [hop(gram, "pipe", j) for j in range(1, sections)]
    grams = [(g, hop(g, "dp", 1)) for g in near]

    coef = chain(partials, squares, docs, grams, head, width, seq)
    line = [coef] + [hop(coef, "dp", k * CORES) for k in range(1, chips)]
    coefs = [line] + [[hop(t, "pipe", j) for t in line] for j in range(1, sections)]
    spread = [tokens] + [[hop(t, "pipe", j) for t in tokens] for j in range(1, sections)]

    half = own[0].shape[0]
    form = rebuild if sections * chips * rows <= 1024 else rebuild_wide
    far, far_grads = form(spread, coefs, other, half, CORES * half, head)
    close, grads = form(spread, coefs, own, 0, CORES * half, head)
    grads = grads + hop(far_grads, "dp", 1)
    out = []
    for k in range(chips):
        for part in (close[k], far[k]):
            part = part.reshape(sections * rows, half)
            out.append(hop(part, "dp", k * CORES) if k else part)
    stored = unpack(out, chips, width)[: batches * seq]
    stored = stored.reshape(1, 1, batches, seq, width)
    return (stored,) + tuple(grads[None, :, i * head : (i + 1) * head] for i in range(4))


def solution(mesh):
    wide = P("dp", None, None, None)
    weight = P("pipe", "dp", None)
    return jax.shard_map(
        shards,
        mesh=mesh,
        in_specs=(wide, P("dp", None, None), wide, weight, weight, weight, weight),
        out_specs=(P("pipe", "dp", None, None, None), weight, weight, weight, weight),
        check_vma=False,
    )
```

```python
import functools

import jax
import jax.numpy as jnp
from jax import lax
from jax.experimental import pallas as pl
from jax.experimental.pallas import tpu as pltpu
from jax.sharding import PartitionSpec as P

BF = jnp.bfloat16
F32 = jnp.float32
NN = (((1,), (0,)), ((), ()))
NT = (((1,), (1,)), ((), ()))
TN = (((0,), (0,)), ((), ()))
VMEM_BYTES = 56 * 2**20
CORES = 2


def dot(a, b, dims=NN):
    return lax.dot_general(a, b, dims, preferred_element_type=F32)


def hop(block, axis, step):
    return lax.ppermute(block, axis, [(i, i ^ step) for i in range(lax.axis_size(axis))])


def place():
    b = lax.axis_index("dp")
    return lax.axis_index("pipe"), b // CORES, b % CORES


def cost(flops, moved):
    return pl.CostEstimate(flops=int(flops), bytes_accessed=int(moved), transcendentals=0)


def vmem(count):
    return [pl.BlockSpec(memory_space=pltpu.VMEM)] * count


def anywhere(count):
    return [pl.BlockSpec(memory_space=pl.ANY)] * count


def across(block, chips):
    groups = [[z * CORES + c for z in range(chips)] for c in range(CORES)]
    return lax.all_to_all(block, "dp", 0, 0, axis_index_groups=groups, tiled=True)


def after(values, *others):
    return lax.optimization_barrier((values, others))[0]


def sides(block):
    return hop(block, "pipe", 1), hop(block, "pipe", 2)


def corner(one, two):
    cut = one.shape[0] // 2
    return hop(one[:cut], "pipe", 2), hop(two[cut:], "pipe", 1)


def fan(block):
    sections = lax.axis_size("pipe")
    if sections != 4:
        return [block] + [hop(block, "pipe", j) for j in range(1, sections)]
    one, two = sides(block)
    return [block, one, two, jnp.concatenate(corner(one, two), axis=0)]


def pack(features, cots, chips):
    _, total, seq, width = features.shape
    group = total // lax.axis_size("pipe")
    eighth = width // (chips * CORES)

    def kernel(x_ref, g_ref, out, squares, sems):
        p, _, c = place()
        copies = []
        for z in range(chips):
            for h in range(CORES):
                start = pl.multiple_of((z * CORES + (c ^ h)) * eighth, eighth)
                for a, ref in enumerate((x_ref, g_ref)):
                    copies.append(
                        pltpu.make_async_copy(
                            ref.at[0, pl.ds(p * group, group), :, pl.ds(start, eighth)],
                            out.at[z, a, :, :, pl.ds(h * eighth, eighth)],
                            sems.at[len(copies)],
                        )
                    )
        for copy in copies:
            copy.start()
        for copy in copies:
            copy.wait()
        for i in range(group):
            total = jnp.zeros((seq, 1), F32)
            for z in range(chips):
                block = out[z, 0, i].astype(F32)
                total = total + jnp.sum(block * block, axis=-1, keepdims=True)
            squares[i * seq : (i + 1) * seq, :] = total

    out, squares = pl.pallas_call(
        kernel,
        name="pack",
        out_shape=(
            jax.ShapeDtypeStruct((chips, 2, group, seq, CORES * eighth), BF),
            jax.ShapeDtypeStruct((group * seq, 1), F32),
        ),
        in_specs=anywhere(2),
        out_specs=tuple(vmem(2)),
        scratch_shapes=[pltpu.SemaphoreType.DMA((chips * CORES * 2,))],
        cost_estimate=cost(0, 8 * group * seq * width * 2),
    )(features, cots)
    return out.reshape(chips, 2, group * seq, CORES * eighth), squares


def unpack(pieces, chips, width):
    rows, eighth = pieces[0].shape

    def kernel(*refs):
        ins, out, sems = refs[:-2], refs[-2], refs[-1]
        _, z, c = place()
        copies = []
        for k in range(chips):
            for h in range(CORES):
                start = pl.multiple_of(((z ^ k) * CORES + (c ^ h)) * eighth, eighth)
                copies.append(
                    pltpu.make_async_copy(
                        ins[k * CORES + h], out.at[:, pl.ds(start, eighth)], sems.at[len(copies)]
                    )
                )
        for copy in copies:
            copy.start()
        for copy in copies:
            copy.wait()

    return pl.pallas_call(
        kernel,
        name="unpack",
        out_shape=jax.ShapeDtypeStruct((rows, width), BF),
        in_specs=vmem(len(pieces)),
        out_specs=pl.BlockSpec(memory_space=pl.ANY),
        scratch_shapes=[pltpu.SemaphoreType.DMA((len(pieces),))],
        cost_estimate=cost(0, 4 * rows * width * 2),
    )(*pieces)


def project(tokens, own, other, wanted, head, apart):
    chips, _, rows, _ = tokens.shape
    given, first = len(own), len(own) - len(wanted)
    half = own[0].shape[0]
    tall = head // rows
    blocks = len(wanted) * (5 + tall)

    def kernel(*refs):
        tok = refs[0]
        ws = refs[1 : 1 + given]
        vs = refs[1 + given : 1 + 2 * given]
        outs = refs[1 + 2 * given :]
        p, z, c = place()
        order = [z ^ k if apart else k for k in range(chips)]
        outs = outs if apart else [outs[0].at[k] for k in range(chips)]
        h = jnp.concatenate([tok[k, 0] for k in order], axis=0)
        g = jnp.concatenate([tok[k, 1] for k in order], axis=0)
        for n in range(len(wanted)):
            w, v = ws[first + n], vs[first + n]
            a = dot(h[:, :half], w[...]) + dot(h[:, half:], v[...])
            b = dot(g[:, :half], w[:, 3 * head :]) + dot(g[:, half:], v[:, 3 * head :])
            for k in range(chips):
                at = slice(k * rows, (k + 1) * rows)
                for i in range(4):
                    part = a[at, i * head : (i + 1) * head]
                    outs[k][n * 5 + i] = part.astype(BF)
                outs[k][n * 5 + 4] = b[at].astype(BF)

        def put(n, low, high, block):
            cols = slice(block * head, (block + 1) * head)
            gram = sum(dot(w[low][:, 3 * head :], w[high][:, cols], TN) for w in (ws, vs))
            for k in range(chips):
                for i in range(tall):
                    part = gram[i * rows : (i + 1) * rows]
                    outs[k][len(wanted) * 5 + n * tall + i] = part.astype(BF)

        for n, j in enumerate(wanted):
            if j == 0:
                put(n, 0, 0, 3)
                continue
            below = p < (p ^ j)
            at = first + n
            for core in range(CORES):
                pl.when(below & (c == core))(functools.partial(put, n, 0, at, core))
                pl.when(jnp.logical_not(below) & (c == core))(
                    functools.partial(put, n, at, 0, CORES + core)
                )

    return pl.pallas_call(
        kernel,
        name="project",
        out_shape=[jax.ShapeDtypeStruct((blocks, rows, head), BF)] * chips
        if apart
        else [jax.ShapeDtypeStruct((chips, blocks, rows, head), BF)],
        in_specs=vmem(1 + 2 * given),
        out_specs=vmem(chips if apart else 1),
        cost_estimate=cost(len(wanted) * 2**31, 4 * given * half * head * 8),
        compiler_params=pltpu.CompilerParams(vmem_limit_bytes=VMEM_BYTES),
    )(tokens, *own, *other)


def chain(rounds, squares, docs, head, width, seq):
    sections = sum(len(wanted) for wanted, _, _ in rounds)
    rows = squares.shape[0]
    lanes = sections * 4 * head
    flat = []
    for _, partials, grams in rounds:
        flat += [*partials] + [g for pair in grams for g in pair]

    def kernel(*refs):
        sq_ref, doc_ref = refs[:2]
        out, a_all, gram = refs[-3:]
        p, _, c = place()
        left = list(refs[2:-3])
        for wanted, partials, grams in rounds:
            a_refs = [left.pop(0) for _ in partials]
            for n, j in enumerate(wanted):
                for i in range(5):
                    at = n * 5 + i
                    if len(a_refs) > 1:
                        parts = [ref[at].astype(F32) for ref in a_refs]
                    else:
                        count = a_refs[0].shape[0]
                        parts = [a_refs[0][z, at].astype(F32) for z in range(count)]
                    a_all[p ^ j, i] = sum(parts)
            for i in range(sections):
                for h in range(CORES):
                    g_ref = left.pop(0)
                    for n, j in enumerate(wanted):
                        one, two = p ^ i, p ^ i ^ j
                        low, high = jnp.minimum(one, two), jnp.maximum(one, two)
                        if j > 0:
                            kind = jnp.where(one < two, 0, CORES) + (c ^ h)
                            gram[low, high, kind] = g_ref[n]
                        elif h == 0:
                            gram[low, high, 3] = g_ref[n]

        def times(m, low, high, kind, dims=NN):
            return dot(m, gram[low, high, kind], dims)

        places_r = lax.broadcasted_iota(jnp.int32, (rows, rows), 0)
        places_c = lax.broadcasted_iota(jnp.int32, (rows, rows), 1)
        across_docs = jnp.broadcast_to(doc_ref[p], (rows, rows))
        down = jnp.sum(jnp.where(places_r == places_c, across_docs, 0), axis=-1, keepdims=True)
        allowed = (places_r >= places_c) & (down == across_docs)
        if rows > seq:
            allowed = allowed & (places_r // seq == places_c // seq)
        scale = head ** (-0.5)

        x = [[a_all[s, i] for i in range(3)] for s in range(sections)]
        ho = [a_all[s, 3] for s in range(sections)]
        bo = [a_all[s, 4] for s in range(sections)]
        norm = sq_ref[...]
        saved = []
        for s in range(sections):
            inv = lax.rsqrt(jnp.maximum(norm, 0.0) / width + 1e-05)
            q, k, v = ((part * inv).astype(BF) for part in x[s])
            scores = jnp.where(allowed, dot(q, k, NT) * scale, -1e30)
            highest = jnp.max(scores, axis=-1, keepdims=True)
            exponent = jnp.where(allowed, jnp.exp(scores - highest), 0.0)
            soft = exponent / jnp.sum(exponent, axis=-1, keepdims=True)
            attend = soft.astype(BF)
            mixed = dot(attend, v).astype(BF)
            saved.append((inv, q, k, v, soft, attend, mixed, list(ho)))
            if s < sections - 1:
                before = ho[s]
                for t in range(s + 1, sections):
                    x[t] = [x[t][i] + times(mixed, s, t, i) for i in range(3)]
                for t in range(sections - 1):
                    if t >= s:
                        ho[t] = ho[t] + times(mixed, s, t, 3)
                    else:
                        ho[t] = ho[t] + times(mixed, t, s, 3, NT)
                wide = mixed.astype(F32)
                norm = norm + jnp.sum(wide * (before + ho[s]), axis=-1, keepdims=True)

        lane = lax.broadcasted_iota(jnp.int32, (rows, head), 1)
        scalars = jnp.zeros((rows, head), F32)
        for s in reversed(range(sections)):
            inv, q, k, v, soft, attend, mixed, along = saved[s]
            d_mixed = bo[s].astype(BF)
            d_attend = dot(d_mixed, v, NT).astype(BF).astype(F32)
            d_values = dot(attend, d_mixed, TN)
            inner = jnp.sum(soft * d_attend, axis=-1, keepdims=True)
            d_scores = (soft * (d_attend - inner) * scale).astype(BF)
            d_query = dot(d_scores, k)
            d_keys = dot(d_scores, q, TN)
            y = [(part * inv).astype(BF) for part in (d_query, d_keys, d_values)]
            inner = sum(y[i].astype(F32) * x[s][i] for i in range(3))
            coef = inv * inv * jnp.sum(inner, axis=-1, keepdims=True) / width
            for t in range(s):
                add = sum(times(y[i], t, s, i, NT) for i in range(3))
                bo[t] = bo[t] + add - coef * along[t]
            at = s * 4 * head
            for i in range(3):
                out[:, at + i * head : at + (i + 1) * head] = y[i]
            out[:, at + 3 * head : at + 4 * head] = mixed
            coarse = coef.astype(BF).astype(F32)
            scalars = jnp.where(lane == 2 * s, coarse, scalars)
            scalars = jnp.where(lane == 2 * s + 1, coef - coarse, scalars)
        out[:, lanes:] = scalars.astype(BF)

    return pl.pallas_call(
        kernel,
        name="chain",
        out_shape=jax.ShapeDtypeStruct((rows, lanes + head), BF),
        in_specs=vmem(2 + len(flat)),
        out_specs=pl.BlockSpec(memory_space=pltpu.VMEM),
        scratch_shapes=[
            pltpu.VMEM((sections, 5, rows, head), F32),
            pltpu.VMEM((sections, sections, 4, head, head), BF),
        ],
        cost_estimate=cost(sections * 2**31, 2**22),
        compiler_params=pltpu.CompilerParams(vmem_limit_bytes=VMEM_BYTES),
    )(squares, docs, *flat)


def rebuild(tokens, coefs, weights, column, head):
    groups, sections = len(tokens), len(weights)
    chips, rows, lanes = coefs[0].shape
    half = weights[0].shape[0]
    some = chips * rows
    count = groups * some
    block = min(256, half)

    def kernel(*refs):
        t_refs, c_refs = refs[:groups], refs[groups : 2 * groups]
        w_refs = refs[2 * groups : 2 * groups + sections]
        outs = refs[2 * groups + sections : 2 * groups + sections + chips]
        grads, left, own_m, edge, h_all, g_all = refs[2 * groups + sections + chips :]
        p, z, _ = place()
        out_w = slice(3 * head, 4 * head)
        qkv_w = slice(0, 3 * head)

        @pl.when(pl.program_id(0) == 0)
        def _():
            for i in range(groups):
                at = pl.ds(i * some, some)
                scalars = c_refs[i][:, :, lanes - head :].reshape(some, head).astype(F32)
                side = lax.broadcasted_iota(jnp.int32, scalars.shape, 1) // 2
                here = jnp.where(side == p, scalars, 0.0)
                here = jnp.sum(here, axis=-1, keepdims=True)
                edge[1, at, :] = jnp.broadcast_to(here, (some, head))
                for j in range(sections):
                    s = p ^ j
                    start = pl.multiple_of(s * 4 * head, 4 * head)
                    both = c_refs[i][:, :, pl.ds(start, 4 * head)].reshape(some, 4 * head)
                    left[j, at, :] = both
                    m = both[:, out_w]

                    def weigh(j=j, s=s, m=m):
                        after = jnp.where((side > s) & (side < sections), scalars, 0.0)
                        share = jnp.sum(after, axis=-1, keepdims=True)
                        left[j, at, out_w] = (-share * m.astype(F32)).astype(BF)
                        if j == 0:
                            edge[0, at, :] = jnp.broadcast_to(share, (some, head))

                    if j == 0:
                        own_m[at, :] = m
                        weigh()
                    else:
                        pl.when(s > p)(weigh)

        for i in range(groups):
            for k in range(chips):
                at = pl.ds(i * some + k * rows, rows)
                h_all[at, :] = t_refs[i][z ^ k, 0].astype(F32)
                g_all[at, :] = t_refs[i][z ^ k, 1].astype(F32)
        for j in range(1, sections):

            @pl.when((p ^ j) < p)
            def _():
                h_all[...] += dot(left[j, :, out_w], w_refs[j][:, out_w], NT)

            @pl.when((p ^ j) > p)
            def _():
                g_all[...] += dot(left[j], w_refs[j][...], NT)

        h = h_all[...]
        y = left[0, :, qkv_w]
        g = g_all[...] + dot(left[0, :, out_w], w_refs[0][:, out_w], NT)
        g = g - edge[0][:, :1] * h
        grads[:, qkv_w] = dot(h.astype(BF), y, TN)
        grads[:, out_w] = dot(g.astype(BF), own_m[...], TN)
        result = (g + dot(y, w_refs[0][:, qkv_w], NT) - edge[1][:, :1] * h).astype(BF)
        for i in range(groups):
            for k in range(chips):
                at = i * some + k * rows
                outs[k][p ^ i] = result[at : at + rows]

    outs = pl.pallas_call(
        kernel,
        name="rebuild",
        grid=(half // block,),
        out_shape=[jax.ShapeDtypeStruct((groups, rows, half), BF)] * chips
        + [jax.ShapeDtypeStruct((half, 4 * head), F32)],
        in_specs=[
            pl.BlockSpec((chips, 2, rows, block), lambda i: (0, 0, 0, i + column // block))
        ]
        * groups
        + vmem(groups)
        + [pl.BlockSpec((block, 4 * head), lambda i: (i, 0))] * sections,
        out_specs=[pl.BlockSpec((groups, rows, block), lambda i: (0, 0, i))] * chips
        + [pl.BlockSpec((block, 4 * head), lambda i: (i, 0))],
        scratch_shapes=[
            pltpu.VMEM((sections, count, 4 * head), BF),
            pltpu.VMEM((count, head), BF),
            pltpu.VMEM((2, count, head), F32),
            pltpu.VMEM((count, block), F32),
            pltpu.VMEM((count, block), F32),
        ],
        cost_estimate=cost(12 * count * half * head * 4 * sections, 2**24),
        compiler_params=pltpu.CompilerParams(vmem_limit_bytes=VMEM_BYTES),
    )(*tokens, *coefs, *weights)
    return outs[:chips], outs[chips]


def rebuild_wide(tokens, coefs, weights, column, head):
    sections = len(weights)
    chips, rows, lanes = coefs[0].shape
    half = weights[0].shape[0]
    p, z, _ = place()
    grads = jnp.zeros((half, 4 * head), F32)
    results = []
    for both, coef in zip(tokens, coefs):
        both, coef, grads = lax.optimization_barrier((both, coef, grads))
        both = jnp.take(both[..., column : column + half], jnp.arange(chips) ^ z, axis=0)
        coef = coef.reshape(chips * rows, lanes)
        scalars = coef[:, lanes - head :].astype(F32)
        side = lax.broadcasted_iota(jnp.int32, scalars.shape, 1) // 2

        def share(s, scalars=scalars, side=side):
            after = jnp.where((side > s) & (side < sections), scalars, 0.0)
            return jnp.sum(after, axis=-1, keepdims=True)

        h = both[:, 0].reshape(chips * rows, half).astype(F32)
        g = both[:, 1].reshape(chips * rows, half).astype(F32)
        for j in range(sections):
            s = p ^ j
            part = lax.dynamic_slice_in_dim(coef, s * 4 * head, 4 * head, axis=1)
            y, m = part[:, : 3 * head], part[:, 3 * head :]
            out_w = weights[j][:, 3 * head :]
            if j == 0:
                own = part
            h = h + dot(jnp.where(s < p, m, jnp.zeros_like(m)), out_w, NT)
            g = g + dot(jnp.where(s > p, y, jnp.zeros_like(y)), weights[j][:, : 3 * head], NT)
            late = jnp.where(s >= p, -share(s) * m.astype(F32), 0.0).astype(BF)
            g = g + dot(late, out_w, NT)
        g = g - share(p) * h
        y, m = own[:, : 3 * head], own[:, 3 * head :]
        here = jnp.sum(jnp.where(side == p, scalars, 0.0), axis=-1, keepdims=True)
        grads = grads + jnp.concatenate(
            [dot(h.astype(BF), y, TN), dot(g.astype(BF), m, TN)], axis=1
        )
        result = (g + dot(y, weights[0][:, : 3 * head], NT) - here * h).astype(BF)
        results.append(result.reshape(chips, rows, half))
    result = jnp.take(jnp.stack(results), jnp.arange(len(tokens)) ^ p, axis=0)
    return [result[:, k] for k in range(chips)], grads


def shards(inputs, segments, cotangent, w_query, w_key, w_value, w_out):
    sections = lax.axis_size("pipe")
    chips = lax.axis_size("dp") // CORES
    head = w_query.shape[2]
    _, batches, seq, width = inputs.shape
    short = -batches % sections
    if short:
        fill = ((0, 0), (0, short), (0, 0), (0, 0))
        inputs, cotangent = jnp.pad(inputs, fill), jnp.pad(cotangent, fill)
        segments = jnp.pad(segments, fill[:3])
    group = inputs.shape[1] // sections
    rows = group * seq

    pieces, squares = pack(inputs, cotangent, chips)
    mine = jnp.concatenate([w_query[0], w_key[0], w_value[0], w_out[0]], axis=1)
    pieces, mine = lax.optimization_barrier((pieces, mine))
    def summed(wanted, part):
        low = len(wanted) * 5
        if len(part) > 1:
            gram = sum(one[low:].astype(F32) for one in part)
        else:
            gram = jnp.sum(part[0][:, low:].astype(F32), axis=0)
        gram = gram.astype(BF).reshape(len(wanted), head, head)
        close = [gram] + [hop(gram, "pipe", j) for j in range(1, sections)]
        return wanted, part, [(g, hop(g, "dp", 1)) for g in close]

    tokens = across(pieces, chips)
    if sections == 4:
        near = hop(mine, "dp", 1)
        one, two = sides(mine)
        low, high = corner(one, two)
        near_one, near_two = (hop(w, "dp", 1) for w in after((one, two), tokens))
        ours, theirs = [mine, one, two], [near, near_one, near_two]
        early = project(tokens, ours, theirs, (0, 1, 2), head, False)
        low, high = after((low, high), *early)
        ours.append(jnp.concatenate([low, high], axis=0))
        theirs.append(hop(ours[3], "dp", 1))
        late = project(tokens, [mine, ours[3]], [near, theirs[3]], (3,), head, True)
        spread = sides(after(tokens, ours[3]))
        spread = [tokens, *spread, jnp.concatenate(corner(*after(spread, late[0])), axis=0)]
        early = summed((0, 1, 2), [across(early[0], chips)])
        late = [late[0]] + [hop(late[k], "dp", k * CORES) for k in range(1, chips)]
        rounds = [early, summed((3,), late)]
    else:
        ours = fan(mine)
        theirs = [hop(w, "dp", 1) for w in ours]
        spread = fan(tokens)
        wanted = tuple(range(sections))
        part = project(tokens, ours, theirs, wanted, head, False)
        rounds = [summed(wanted, [across(part[0], chips)])]

    docs = segments.reshape(sections, 1, rows)
    squares, *spread = lax.optimization_barrier((squares, *spread))
    coef = chain(rounds, squares, docs, head, width, seq)
    coef = jnp.stack([coef] + [hop(coef, "dp", k * CORES) for k in range(1, chips)])
    coefs = fan(coef)

    half = mine.shape[0]
    form = rebuild if sections * chips * rows <= 1024 else rebuild_wide
    far, far_grads = form(spread, coefs, theirs, half, head)
    close, grads = form(spread, coefs, ours, 0, head)
    grads = grads + hop(far_grads, "dp", 1)
    grads = [grads[None, :, i * head : (i + 1) * head] for i in range(4)]
    def sent(pieces):
        pieces = [part.reshape(sections * rows, half) for part in pieces]
        return [pieces[0]] + [hop(pieces[k], "dp", k * CORES) for k in range(1, chips)]

    far = sent(far)
    close = sent(after(close, far))
    out = [part for pair in zip(close, far) for part in pair]
    out, grads = lax.optimization_barrier((out, grads))
    stored = unpack(out, chips, width)[: batches * seq]
    return (stored.reshape(1, 1, batches, seq, width), *grads)


def solution(mesh):
    wide = P("dp", None, None, None)
    weight = P("pipe", "dp", None)
    return jax.shard_map(
        shards,
        mesh=mesh,
        in_specs=(wide, P("dp", None, None), wide, weight, weight, weight, weight),
        out_specs=(P("pipe", "dp", None, None, None), weight, weight, weight, weight),
        check_vma=False,
    )
```

```python
import functools

import jax
import jax.numpy as jnp
from jax import lax
from jax.experimental import pallas as pl
from jax.experimental.pallas import tpu as pltpu
from jax.sharding import PartitionSpec as P

BF = jnp.bfloat16
F32 = jnp.float32
NN = (((1,), (0,)), ((), ()))
NT = (((1,), (1,)), ((), ()))
TN = (((0,), (0,)), ((), ()))
VMEM_BYTES = 56 * 2**20
CORES = 2


def dot(a, b, dims=NN):
    return lax.dot_general(a, b, dims, preferred_element_type=F32)


def hop(block, axis, step):
    return lax.ppermute(block, axis, [(i, i ^ step) for i in range(lax.axis_size(axis))])


def place():
    b = lax.axis_index("dp")
    return lax.axis_index("pipe"), b // CORES, b % CORES


def cost(flops, moved):
    return pl.CostEstimate(flops=int(flops), bytes_accessed=int(moved), transcendentals=0)


def vmem(count):
    return [pl.BlockSpec(memory_space=pltpu.VMEM)] * count


def anywhere(count):
    return [pl.BlockSpec(memory_space=pl.ANY)] * count


def across(block, chips):
    groups = [[z * CORES + c for z in range(chips)] for c in range(CORES)]
    return lax.all_to_all(block, "dp", 0, 0, axis_index_groups=groups, tiled=True)


def after(values, *others):
    return lax.optimization_barrier((values, others))[0]


def sides(block):
    return hop(block, "pipe", 1), hop(block, "pipe", 2)


def corner(one, two):
    cut = one.shape[0] // 2
    return hop(one[:cut], "pipe", 2), hop(two[cut:], "pipe", 1)


def fan(block):
    sections = lax.axis_size("pipe")
    if sections != 4:
        return [block] + [hop(block, "pipe", j) for j in range(1, sections)]
    one, two = sides(block)
    return [block, one, two, jnp.concatenate(corner(one, two), axis=0)]


def pack(features, cots, chips):
    _, total, seq, width = features.shape
    group = total // lax.axis_size("pipe")
    eighth = width // (chips * CORES)

    def kernel(x_ref, g_ref, out, squares, sems):
        p, _, c = place()
        copies = []
        for z in range(chips):
            for h in range(CORES):
                start = pl.multiple_of((z * CORES + (c ^ h)) * eighth, eighth)
                for a, ref in enumerate((x_ref, g_ref)):
                    copies.append(
                        pltpu.make_async_copy(
                            ref.at[0, pl.ds(p * group, group), :, pl.ds(start, eighth)],
                            out.at[z, a, :, :, pl.ds(h * eighth, eighth)],
                            sems.at[len(copies)],
                        )
                    )
        for copy in copies:
            copy.start()
        for copy in copies:
            copy.wait()
        for i in range(group):
            total = jnp.zeros((seq, 1), F32)
            for z in range(chips):
                block = out[z, 0, i].astype(F32)
                total = total + jnp.sum(block * block, axis=-1, keepdims=True)
            squares[i * seq : (i + 1) * seq, :] = total

    out, squares = pl.pallas_call(
        kernel,
        name="pack",
        out_shape=(
            jax.ShapeDtypeStruct((chips, 2, group, seq, CORES * eighth), BF),
            jax.ShapeDtypeStruct((group * seq, 1), F32),
        ),
        in_specs=anywhere(2),
        out_specs=tuple(vmem(2)),
        scratch_shapes=[pltpu.SemaphoreType.DMA((chips * CORES * 2,))],
        cost_estimate=cost(0, 8 * group * seq * width * 2),
    )(features, cots)
    return out.reshape(chips, 2, group * seq, CORES * eighth), squares


def unpack(parts, width):
    flat = [array for arrays, _, _ in parts for array in arrays]
    rows, chips = flat[0].shape[-2], lax.axis_size("dp") // CORES
    eighth = width // (chips * CORES)
    sections = sum(len(groups) * len(halves) for _, groups, halves in parts) // CORES

    def kernel(*refs):
        ins, out, sems = list(refs[:-2]), refs[-2], refs[-1]
        p, z, c = place()
        copies = []
        for arrays, groups, halves in parts:
            held = [ins.pop(0) for _ in arrays]
            for k in range(chips):
                chip, ref = (z ^ k, held[k]) if len(held) > 1 else (k, held[0].at[k])
                for n, group in enumerate(groups):
                    row = pl.multiple_of((p ^ group) * rows, rows)
                    for i, h in enumerate(halves):
                        start = pl.multiple_of((chip * CORES + (c ^ h)) * eighth, eighth)
                        copies.append(
                            pltpu.make_async_copy(
                                ref.at[n, :, pl.ds(i * eighth, eighth)],
                                out.at[pl.ds(row, rows), pl.ds(start, eighth)],
                                sems.at[len(copies)],
                            )
                        )
        for copy in copies:
            copy.start()
        for copy in copies:
            copy.wait()

    return pl.pallas_call(
        kernel,
        name="unpack",
        out_shape=jax.ShapeDtypeStruct((sections * rows, width), BF),
        in_specs=vmem(len(flat)),
        out_specs=pl.BlockSpec(memory_space=pl.ANY),
        scratch_shapes=[pltpu.SemaphoreType.DMA((sections * chips * CORES,))],
        cost_estimate=cost(0, 4 * sections * rows * width * 2),
    )(*flat)


def project(tokens, own, other, wanted, head, apart):
    chips, _, rows, _ = tokens.shape
    given, first = len(own), len(own) - len(wanted)
    half = own[0].shape[0]
    tall = head // rows
    blocks = len(wanted) * (5 + tall)

    def kernel(*refs):
        tok = refs[0]
        ws = refs[1 : 1 + given]
        vs = refs[1 + given : 1 + 2 * given]
        outs = refs[1 + 2 * given :]
        p, z, c = place()
        order = [z ^ k if apart else k for k in range(chips)]
        outs = outs if apart else [outs[0].at[k] for k in range(chips)]
        h = jnp.concatenate([tok[k, 0] for k in order], axis=0)
        g = jnp.concatenate([tok[k, 1] for k in order], axis=0)
        for n in range(len(wanted)):
            w, v = ws[first + n], vs[first + n]
            a = dot(h[:, :half], w[...]) + dot(h[:, half:], v[...])
            b = dot(g[:, :half], w[:, 3 * head :]) + dot(g[:, half:], v[:, 3 * head :])
            for k in range(chips):
                at = slice(k * rows, (k + 1) * rows)
                for i in range(4):
                    part = a[at, i * head : (i + 1) * head]
                    outs[k][n * 5 + i] = part.astype(BF)
                outs[k][n * 5 + 4] = b[at].astype(BF)

        def put(n, low, high, block):
            cols = slice(block * head, (block + 1) * head)
            gram = sum(dot(w[low][:, 3 * head :], w[high][:, cols], TN) for w in (ws, vs))
            for k in range(chips):
                for i in range(tall):
                    part = gram[i * rows : (i + 1) * rows]
                    outs[k][len(wanted) * 5 + n * tall + i] = part.astype(BF)

        for n, j in enumerate(wanted):
            if j == 0:
                put(n, 0, 0, 3)
                continue
            below = p < (p ^ j)
            at = first + n
            for core in range(CORES):
                pl.when(below & (c == core))(functools.partial(put, n, 0, at, core))
                pl.when(jnp.logical_not(below) & (c == core))(
                    functools.partial(put, n, at, 0, CORES + core)
                )

    return pl.pallas_call(
        kernel,
        name="project",
        out_shape=[jax.ShapeDtypeStruct((blocks, rows, head), BF)] * chips
        if apart
        else [jax.ShapeDtypeStruct((chips, blocks, rows, head), BF)],
        in_specs=vmem(1 + 2 * given),
        out_specs=vmem(chips if apart else 1),
        cost_estimate=cost(len(wanted) * 2**31, 4 * given * half * head * 8),
        compiler_params=pltpu.CompilerParams(vmem_limit_bytes=VMEM_BYTES),
    )(tokens, *own, *other)


def chain(rounds, squares, docs, head, width, seq):
    sections = sum(len(wanted) for wanted, _, _ in rounds)
    rows = squares.shape[0]
    lanes = sections * 4 * head
    flat = []
    for _, partials, grams in rounds:
        flat += [*partials] + [g for pair in grams for g in pair]

    def kernel(*refs):
        sq_ref, doc_ref = refs[:2]
        out, a_all, gram = refs[-3:]
        p, _, c = place()
        left = list(refs[2:-3])
        for wanted, partials, grams in rounds:
            a_refs = [left.pop(0) for _ in partials]
            for n, j in enumerate(wanted):
                for i in range(5):
                    at = n * 5 + i
                    if len(a_refs) > 1:
                        parts = [ref[at].astype(F32) for ref in a_refs]
                    else:
                        count = a_refs[0].shape[0]
                        parts = [a_refs[0][z, at].astype(F32) for z in range(count)]
                    a_all[p ^ j, i] = sum(parts)
            for i in range(sections):
                for h in range(CORES):
                    g_ref = left.pop(0)
                    for n, j in enumerate(wanted):
                        one, two = p ^ i, p ^ i ^ j
                        low, high = jnp.minimum(one, two), jnp.maximum(one, two)
                        if j > 0:
                            kind = jnp.where(one < two, 0, CORES) + (c ^ h)
                            gram[low, high, kind] = g_ref[n]
                        elif h == 0:
                            gram[low, high, 3] = g_ref[n]

        def times(m, low, high, kind, dims=NN):
            return dot(m, gram[low, high, kind], dims)

        places_r = lax.broadcasted_iota(jnp.int32, (rows, rows), 0)
        places_c = lax.broadcasted_iota(jnp.int32, (rows, rows), 1)
        across_docs = jnp.broadcast_to(doc_ref[p], (rows, rows))
        down = jnp.sum(jnp.where(places_r == places_c, across_docs, 0), axis=-1, keepdims=True)
        allowed = (places_r >= places_c) & (down == across_docs)
        if rows > seq:
            allowed = allowed & (places_r // seq == places_c // seq)
        scale = head ** (-0.5)

        x = [[a_all[s, i] for i in range(3)] for s in range(sections)]
        ho = [a_all[s, 3] for s in range(sections)]
        bo = [a_all[s, 4] for s in range(sections)]
        norm = sq_ref[...]
        saved = []
        for s in range(sections):
            inv = lax.rsqrt(jnp.maximum(norm, 0.0) / width + 1e-05)
            q, k, v = ((part * inv).astype(BF) for part in x[s])
            scores = jnp.where(allowed, dot(q, k, NT) * scale, -1e30)
            highest = jnp.max(scores, axis=-1, keepdims=True)
            exponent = jnp.where(allowed, jnp.exp(scores - highest), 0.0)
            soft = exponent / jnp.sum(exponent, axis=-1, keepdims=True)
            attend = soft.astype(BF)
            mixed = dot(attend, v).astype(BF)
            saved.append((inv, q, k, v, soft, attend, mixed, list(ho)))
            if s < sections - 1:
                before = ho[s]
                for t in range(s + 1, sections):
                    x[t] = [x[t][i] + times(mixed, s, t, i) for i in range(3)]
                for t in range(sections - 1):
                    if t >= s:
                        ho[t] = ho[t] + times(mixed, s, t, 3)
                    else:
                        ho[t] = ho[t] + times(mixed, t, s, 3, NT)
                wide = mixed.astype(F32)
                norm = norm + jnp.sum(wide * (before + ho[s]), axis=-1, keepdims=True)

        lane = lax.broadcasted_iota(jnp.int32, (rows, head), 1)
        scalars = jnp.zeros((rows, head), F32)
        for s in reversed(range(sections)):
            inv, q, k, v, soft, attend, mixed, along = saved[s]
            d_mixed = bo[s].astype(BF)
            d_attend = dot(d_mixed, v, NT).astype(BF).astype(F32)
            d_values = dot(attend, d_mixed, TN)
            inner = jnp.sum(soft * d_attend, axis=-1, keepdims=True)
            d_scores = (soft * (d_attend - inner) * scale).astype(BF)
            d_query = dot(d_scores, k)
            d_keys = dot(d_scores, q, TN)
            y = [(part * inv).astype(BF) for part in (d_query, d_keys, d_values)]
            inner = sum(y[i].astype(F32) * x[s][i] for i in range(3))
            coef = inv * inv * jnp.sum(inner, axis=-1, keepdims=True) / width
            for t in range(s):
                add = sum(times(y[i], t, s, i, NT) for i in range(3))
                bo[t] = bo[t] + add - coef * along[t]
            at = s * 4 * head
            for i in range(3):
                out[:, at + i * head : at + (i + 1) * head] = y[i]
            out[:, at + 3 * head : at + 4 * head] = mixed
            coarse = coef.astype(BF).astype(F32)
            scalars = jnp.where(lane == 2 * s, coarse, scalars)
            scalars = jnp.where(lane == 2 * s + 1, coef - coarse, scalars)
        out[:, lanes:] = scalars.astype(BF)

    return pl.pallas_call(
        kernel,
        name="chain",
        out_shape=jax.ShapeDtypeStruct((rows, lanes + head), BF),
        in_specs=vmem(2 + len(flat)),
        out_specs=pl.BlockSpec(memory_space=pltpu.VMEM),
        scratch_shapes=[
            pltpu.VMEM((sections, 5, rows, head), F32),
            pltpu.VMEM((sections, sections, 4, head, head), BF),
        ],
        cost_estimate=cost(sections * 2**31, 2**22),
        compiler_params=pltpu.CompilerParams(vmem_limit_bytes=VMEM_BYTES),
    )(squares, docs, *flat)


def rebuild(tokens, coefs, weights, halves, head, apart):
    groups, sections = len(coefs), len(weights[0])
    chips, rows, lanes = coefs[0].shape
    half = weights[0][0].shape[0]
    some = chips * rows
    count = groups * some
    block = min(512, half)
    steps = half // block
    wide = len(halves) * half
    chosen = [weights[h] for h in halves]

    def kernel(*refs):
        t_refs, c_refs = refs[:groups], refs[groups : 2 * groups]
        w_refs = refs[2 * groups : 2 * groups + len(halves) * sections]
        outs = refs[2 * groups + len(halves) * sections : -7]
        h_out, g_out, left, edge, h_all, g_all, kept = refs[-7:]
        p, z, _ = place()
        outs = outs if apart else [outs[0].at[z ^ k] for k in range(chips)]
        out_w = slice(3 * head, 4 * head)
        qkv_w = slice(0, 3 * head)

        @pl.when(pl.program_id(0) == 0)
        def _():
            for i in range(groups):
                at = pl.ds(i * some, some)
                scalars = c_refs[i][:, :, lanes - head :].reshape(some, head).astype(F32)
                side = lax.broadcasted_iota(jnp.int32, scalars.shape, 1) // 2
                here = jnp.where(side == p, scalars, 0.0)
                here = jnp.sum(here, axis=-1, keepdims=True)
                edge[1, at, :] = jnp.broadcast_to(here, (some, head))
                for j in range(sections):
                    s = p ^ j
                    start = pl.multiple_of(s * 4 * head, 4 * head)
                    both = c_refs[i][:, :, pl.ds(start, 4 * head)].reshape(some, 4 * head)
                    left[j, at, :] = both
                    m = both[:, out_w]

                    def weigh(j=j, s=s, m=m):
                        later = jnp.where((side > s) & (side < sections), scalars, 0.0)
                        share = jnp.sum(later, axis=-1, keepdims=True)
                        left[j, at, out_w] = (-share * m.astype(F32)).astype(BF)
                        if j == 0:
                            edge[0, at, :] = jnp.broadcast_to(share, (some, head))

                    if j == 0:
                        weigh()
                    else:
                        pl.when(s > p)(weigh)

        for i in range(groups):
            for k in range(chips):
                at = pl.ds(i * some + k * rows, rows)
                h_all[at, :] = t_refs[i][z ^ k, 0].astype(F32)
                g_all[at, :] = t_refs[i][z ^ k, 1].astype(F32)

        def add(held):
            for j in range(1, sections):

                @pl.when((p ^ j) < p)
                def _():
                    h_all[...] += dot(left[j, :, out_w], held[j][:, out_w], NT)

                @pl.when((p ^ j) > p)
                def _():
                    g_all[...] += dot(left[j], held[j][...], NT)

            g_all[...] += dot(left[0, :, out_w], held[0][:, out_w], NT)
            kept[...] = dot(left[0, :, qkv_w], held[0][:, qkv_w], NT)

        for n in range(len(halves)):
            held = w_refs[n * sections : (n + 1) * sections]
            if len(halves) == 1:
                add(held)
            else:
                pl.when(pl.program_id(0) // steps == n)(functools.partial(add, held))

        h = h_all[...]
        g = g_all[...] - edge[0][:, :1] * h
        h_out[...] = h.astype(BF)
        g_out[...] = g.astype(BF)
        result = (g + kept[...] - edge[1][:, :1] * h).astype(BF)
        for i in range(groups):
            for k in range(chips):
                at = i * some + k * rows
                outs[k][i] = result[at : at + rows]

    if apart:
        shapes = [(groups, rows, wide)] * chips
        specs = [pl.BlockSpec((groups, rows, block), lambda i: (0, 0, i))] * chips
    else:
        shapes = [(chips, groups, rows, wide)]
        specs = [pl.BlockSpec((chips, groups, rows, block), lambda i: (0, 0, 0, i))]
    first = halves[0] * steps
    outs = pl.pallas_call(
        kernel,
        name="rebuild",
        grid=(wide // block,),
        out_shape=[jax.ShapeDtypeStruct(shape, BF) for shape in [*shapes] + [(count, wide)] * 2],
        in_specs=[pl.BlockSpec((chips, 2, rows, block), lambda i: (0, 0, 0, i + first))] * groups
        + vmem(groups)
        + [
            pl.BlockSpec(
                (block, 4 * head), lambda i, n=n: (jnp.clip(i - n * steps, 0, steps - 1), 0)
            )
            for n in range(len(halves))
            for _ in range(sections)
        ],
        out_specs=specs + [pl.BlockSpec((count, block), lambda i: (0, i))] * 2,
        scratch_shapes=[
            pltpu.VMEM((sections, count, 4 * head), BF),
            pltpu.VMEM((2, count, head), F32),
            pltpu.VMEM((count, block), F32),
            pltpu.VMEM((count, block), F32),
            pltpu.VMEM((count, block), F32),
        ],
        cost_estimate=cost(12 * count * wide * head * 4 * sections, 2**24),
        compiler_params=pltpu.CompilerParams(vmem_limit_bytes=VMEM_BYTES),
    )(*tokens, *coefs, *[w for held in chosen for w in held])
    return outs[:-2], outs[-2], outs[-1]


def gradients(built, coefs, order, half, h, head, dtype):
    chips, rows, lanes = coefs[0].shape
    some = chips * rows
    block = min(512, half)
    taken = [(hs, gs, halves.index(h)) for hs, gs, halves in built if h in halves]

    def kernel(*refs):
        n = len(taken)
        h_refs, g_refs, c_refs, out = refs[:n], refs[n : 2 * n], refs[2 * n : -1], refs[-1]
        start = pl.multiple_of(lax.axis_index("pipe") * 4 * head, 4 * head)
        own = [c_refs[i][:, :, pl.ds(start, 4 * head)].reshape(some, 4 * head) for i in order]
        own = jnp.concatenate(own, axis=0)
        hs = jnp.concatenate([ref[...] for ref in h_refs], axis=0)
        gs = jnp.concatenate([ref[...] for ref in g_refs], axis=0)
        out[:, : 3 * head] = dot(hs, own[:, : 3 * head], TN).astype(dtype)
        out[:, 3 * head :] = dot(gs, own[:, 3 * head :], TN).astype(dtype)

    specs = [
        pl.BlockSpec((hs.shape[0], block), lambda i, at=at: (0, i + at * (half // block)))
        for hs, _, at in taken
    ]
    return pl.pallas_call(
        kernel,
        name="gradients",
        grid=(half // block,),
        out_shape=jax.ShapeDtypeStruct((half, 4 * head), dtype),
        in_specs=specs * 2 + vmem(len(coefs)),
        out_specs=pl.BlockSpec((block, 4 * head), lambda i: (i, 0)),
        cost_estimate=cost(2**33, 2**23),
        compiler_params=pltpu.CompilerParams(vmem_limit_bytes=VMEM_BYTES),
    )(*[hs for hs, _, _ in taken], *[gs for _, gs, _ in taken], *coefs)


def rebuild_wide(tokens, coefs, weights, column, head):
    sections = len(weights)
    chips, rows, lanes = coefs[0].shape
    half = weights[0].shape[0]
    p, z, _ = place()
    grads = jnp.zeros((half, 4 * head), F32)
    results = []
    for both, coef in zip(tokens, coefs):
        both, coef, grads = lax.optimization_barrier((both, coef, grads))
        both = jnp.take(both[..., column : column + half], jnp.arange(chips) ^ z, axis=0)
        coef = coef.reshape(chips * rows, lanes)
        scalars = coef[:, lanes - head :].astype(F32)
        side = lax.broadcasted_iota(jnp.int32, scalars.shape, 1) // 2

        def share(s, scalars=scalars, side=side):
            after = jnp.where((side > s) & (side < sections), scalars, 0.0)
            return jnp.sum(after, axis=-1, keepdims=True)

        h = both[:, 0].reshape(chips * rows, half).astype(F32)
        g = both[:, 1].reshape(chips * rows, half).astype(F32)
        for j in range(sections):
            s = p ^ j
            part = lax.dynamic_slice_in_dim(coef, s * 4 * head, 4 * head, axis=1)
            y, m = part[:, : 3 * head], part[:, 3 * head :]
            out_w = weights[j][:, 3 * head :]
            if j == 0:
                own = part
            h = h + dot(jnp.where(s < p, m, jnp.zeros_like(m)), out_w, NT)
            g = g + dot(jnp.where(s > p, y, jnp.zeros_like(y)), weights[j][:, : 3 * head], NT)
            late = jnp.where(s >= p, -share(s) * m.astype(F32), 0.0).astype(BF)
            g = g + dot(late, out_w, NT)
        g = g - share(p) * h
        y, m = own[:, : 3 * head], own[:, 3 * head :]
        here = jnp.sum(jnp.where(side == p, scalars, 0.0), axis=-1, keepdims=True)
        grads = grads + jnp.concatenate(
            [dot(h.astype(BF), y, TN), dot(g.astype(BF), m, TN)], axis=1
        )
        result = (g + dot(y, weights[0][:, : 3 * head], NT) - here * h).astype(BF)
        results.append(result.reshape(chips, rows, half))
    result = jnp.stack(results, axis=1)
    return jnp.take(result, jnp.arange(chips) ^ z, axis=0), grads


def shards(inputs, segments, cotangent, w_query, w_key, w_value, w_out):
    sections = lax.axis_size("pipe")
    chips = lax.axis_size("dp") // CORES
    head = w_query.shape[2]
    _, batches, seq, width = inputs.shape
    short = -batches % sections
    if short:
        fill = ((0, 0), (0, short), (0, 0), (0, 0))
        inputs, cotangent = jnp.pad(inputs, fill), jnp.pad(cotangent, fill)
        segments = jnp.pad(segments, fill[:3])
    group = inputs.shape[1] // sections
    rows = group * seq

    pieces, squares = pack(inputs, cotangent, chips)
    mine = jnp.concatenate([w_query[0], w_key[0], w_value[0], w_out[0]], axis=1)
    pieces, mine = lax.optimization_barrier((pieces, mine))
    def summed(wanted, part):
        low = len(wanted) * 5
        if len(part) > 1:
            gram = sum(one[low:].astype(F32) for one in part)
        else:
            gram = jnp.sum(part[0][:, low:].astype(F32), axis=0)
        gram = gram.astype(BF).reshape(len(wanted), head, head)
        close = [gram] + [hop(gram, "pipe", j) for j in range(1, sections)]
        return wanted, part, [(g, hop(g, "dp", 1)) for g in close]

    tokens = across(pieces, chips)
    if sections == 4:
        near = hop(mine, "dp", 1)
        one, two = sides(mine)
        low, high = corner(one, two)
        near_one, near_two = (hop(w, "dp", 1) for w in after((one, two), tokens))
        ours, theirs = [mine, one, two], [near, near_one, near_two]
        early = project(tokens, ours, theirs, (0, 1, 2), head, False)
        low, high = after((low, high), *early)
        ours.append(jnp.concatenate([low, high], axis=0))
        theirs.append(hop(ours[3], "dp", 1))
        late = project(tokens, [mine, ours[3]], [near, theirs[3]], (3,), head, False)
        spread = sides(after(tokens, ours[3]))
        early = summed((0, 1, 2), [across(early[0], chips)])
        late = across(after(late[0], early[1]), chips)
        late = summed((3,), [after(late, early[2][0])])
        rounds = [early, late]
        plane = [pair[0] for pair in early[2]]
        spread = [tokens, *spread, jnp.concatenate(corner(*after(spread, plane)), axis=0)]
    else:
        ours = fan(mine)
        theirs = [hop(w, "dp", 1) for w in ours]
        spread = fan(tokens)
        wanted = tuple(range(sections))
        part = project(tokens, ours, theirs, wanted, head, False)
        rounds = [summed(wanted, [across(part[0], chips)])]

    docs = segments.reshape(sections, 1, rows)
    coef = chain(rounds, squares, docs, head, width, seq)
    coef = jnp.stack([coef] + [hop(coef, "dp", k * CORES) for k in range(1, chips)])

    half = mine.shape[0]
    if sections == 4:
        sent, built, raw = [], [], []

        def task(groups, halves, apart, before=(), between=()):
            token, scale = [spread[i] for i in groups], [coefs[i] for i in groups]
            token, scale = after((token, scale), *before)
            part, hs, gs = rebuild(token, scale, (ours, theirs), halves, head, apart)
            built.append((hs, gs, halves))
            raw.append(part)
            part = after(part, *between)
            if apart:
                part = [part[0]] + [hop(part[k], "dp", k * CORES) for k in range(1, chips)]
            else:
                part = [across(part[0], chips)]
            sent.append((part, groups, halves))

        coefs = [coef]
        task((0,), (0, 1), False)
        coefs += sides(after(coef, spread[3]))
        task((1, 2), (1,), True)
        task((1, 2), (0,), False, before=sent[0][0])
        coefs.append(jnp.concatenate(corner(*coefs[1:]), axis=0))
        task((3,), (0, 1), True, before=(sent[1][0], raw[2]), between=sent[1][0])
        halves_of = [halves for _, _, halves in built]
        token = hop(raw[3][0][:1, :8, :head], "dp", 1)
        arrays = after([pair[:2] for pair in built], sent[2][0], token)
        built = [(*pair, halves) for pair, halves in zip(arrays, halves_of)]
        far_grads = gradients(built, coefs, range(4), half, 1, head, BF)
        grads = gradients(built, coefs, range(4), half, 0, head, F32)
    else:
        coefs = fan(coef)
        far, far_grads = rebuild_wide(spread, coefs, theirs, half, head)
        close, grads = rebuild_wide(spread, coefs, ours, 0, head)
        order = tuple(range(sections))
        sent = [([across(far, chips)], order, (1,)), ([across(close, chips)], order, (0,))]
    grads = grads + hop(far_grads, "dp", 1).astype(F32)
    grads = [grads[None, :, i * head : (i + 1) * head] for i in range(4)]
    arrays, grads = lax.optimization_barrier(([part for part, _, _ in sent], grads))
    sent = [(part, groups, halves) for part, (_, groups, halves) in zip(arrays, sent)]
    stored = unpack(sent, width)[: batches * seq]
    return (stored.reshape(1, 1, batches, seq, width), *grads)


def solution(mesh):
    wide = P("dp", None, None, None)
    weight = P("pipe", "dp", None)
    return jax.shard_map(
        shards,
        mesh=mesh,
        in_specs=(wide, P("dp", None, None), wide, weight, weight, weight, weight),
        out_specs=(P("pipe", "dp", None, None, None), weight, weight, weight, weight),
        check_vma=False,
    )
```

```python
import functools

import jax
import jax.numpy as jnp
from jax import lax
from jax.experimental import pallas as pl
from jax.experimental.pallas import tpu as pltpu
from jax.sharding import PartitionSpec as P

BF = jnp.bfloat16
F32 = jnp.float32
NN = (((1,), (0,)), ((), ()))
NT = (((1,), (1,)), ((), ()))
TN = (((0,), (0,)), ((), ()))
VMEM_BYTES = 56 * 2**20
CORES = 2


def dot(a, b, dims=NN):
    return lax.dot_general(a, b, dims, preferred_element_type=F32)


def hop(block, axis, step):
    return lax.ppermute(block, axis, [(i, i ^ step) for i in range(lax.axis_size(axis))])


def place():
    b = lax.axis_index("dp")
    return lax.axis_index("pipe"), b // CORES, b % CORES


def cost(flops, moved):
    return pl.CostEstimate(flops=int(flops), bytes_accessed=int(moved), transcendentals=0)


def vmem(count):
    return [pl.BlockSpec(memory_space=pltpu.VMEM)] * count


def anywhere(count):
    return [pl.BlockSpec(memory_space=pl.ANY)] * count


def across(block, chips):
    groups = [[z * CORES + c for z in range(chips)] for c in range(CORES)]
    return lax.all_to_all(block, "dp", 0, 0, axis_index_groups=groups, tiled=True)


def after(values, *others):
    return lax.optimization_barrier((values, others))[0]


def sides(block):
    return hop(block, "pipe", 1), hop(block, "pipe", 2)


def corner(one, two):
    cut = one.shape[0] // 2
    return hop(one[:cut], "pipe", 2), hop(two[cut:], "pipe", 1)


def fan(block):
    sections = lax.axis_size("pipe")
    if sections != 4:
        return [block] + [hop(block, "pipe", j) for j in range(1, sections)]
    one, two = sides(block)
    return [block, one, two, jnp.concatenate(corner(one, two), axis=0)]


def pack(features, cots, chips):
    _, total, seq, width = features.shape
    group = total // lax.axis_size("pipe")
    eighth = width // (chips * CORES)

    def kernel(x_ref, g_ref, out, squares, sems):
        p, _, c = place()
        copies = []
        for z in range(chips):
            for h in range(CORES):
                start = pl.multiple_of((z * CORES + (c ^ h)) * eighth, eighth)
                for a, ref in enumerate((x_ref, g_ref)):
                    copies.append(
                        pltpu.make_async_copy(
                            ref.at[0, pl.ds(p * group, group), :, pl.ds(start, eighth)],
                            out.at[z, a, :, :, pl.ds(h * eighth, eighth)],
                            sems.at[len(copies)],
                        )
                    )
        for copy in copies:
            copy.start()
        for copy in copies:
            copy.wait()
        for i in range(group):
            total = jnp.zeros((seq, 1), F32)
            for z in range(chips):
                block = out[z, 0, i].astype(F32)
                total = total + jnp.sum(block * block, axis=-1, keepdims=True)
            squares[i * seq : (i + 1) * seq, :] = total

    out, squares = pl.pallas_call(
        kernel,
        name="pack",
        out_shape=(
            jax.ShapeDtypeStruct((chips, 2, group, seq, CORES * eighth), BF),
            jax.ShapeDtypeStruct((group * seq, 1), F32),
        ),
        in_specs=anywhere(2),
        out_specs=tuple(vmem(2)),
        scratch_shapes=[pltpu.SemaphoreType.DMA((chips * CORES * 2,))],
        cost_estimate=cost(0, 8 * group * seq * width * 2),
    )(features, cots)
    return out.reshape(chips, 2, group * seq, CORES * eighth), squares


def unpack(parts, width):
    flat = [array for arrays, _, _ in parts for array in arrays]
    rows, chips = flat[0].shape[-2], lax.axis_size("dp") // CORES
    eighth = width // (chips * CORES)
    sections = sum(len(groups) * len(halves) for _, groups, halves in parts) // CORES

    def kernel(*refs):
        ins, out, sems = list(refs[:-2]), refs[-2], refs[-1]
        p, z, c = place()
        copies = []
        for arrays, groups, halves in parts:
            held = [ins.pop(0) for _ in arrays]
            for k in range(chips):
                chip, ref = (z ^ k, held[k]) if len(held) > 1 else (k, held[0].at[k])
                for n, group in enumerate(groups):
                    row = pl.multiple_of((p ^ group) * rows, rows)
                    for i, h in enumerate(halves):
                        start = pl.multiple_of((chip * CORES + (c ^ h)) * eighth, eighth)
                        copies.append(
                            pltpu.make_async_copy(
                                ref.at[n, :, pl.ds(i * eighth, eighth)],
                                out.at[pl.ds(row, rows), pl.ds(start, eighth)],
                                sems.at[len(copies)],
                            )
                        )
        for copy in copies:
            copy.start()
        for copy in copies:
            copy.wait()

    return pl.pallas_call(
        kernel,
        name="unpack",
        out_shape=jax.ShapeDtypeStruct((sections * rows, width), BF),
        in_specs=vmem(len(flat)),
        out_specs=pl.BlockSpec(memory_space=pl.ANY),
        scratch_shapes=[pltpu.SemaphoreType.DMA((sections * chips * CORES,))],
        cost_estimate=cost(0, 4 * sections * rows * width * 2),
    )(*flat)


def project(tokens, own, other, wanted, head, apart):
    chips, _, rows, _ = tokens.shape
    given, first = len(own), len(own) - len(wanted)
    half = own[0].shape[0]
    tall = head // rows
    blocks = len(wanted) * (5 + tall)

    def kernel(*refs):
        tok = refs[0]
        ws = refs[1 : 1 + given]
        vs = refs[1 + given : 1 + 2 * given]
        outs = refs[1 + 2 * given :]
        p, z, c = place()
        order = [z ^ k if apart else k for k in range(chips)]
        outs = outs if apart else [outs[0].at[k] for k in range(chips)]
        h = jnp.concatenate([tok[k, 0] for k in order], axis=0)
        g = jnp.concatenate([tok[k, 1] for k in order], axis=0)
        for n in range(len(wanted)):
            w, v = ws[first + n], vs[first + n]
            a = dot(h[:, :half], w[...]) + dot(h[:, half:], v[...])
            b = dot(g[:, :half], w[:, 3 * head :]) + dot(g[:, half:], v[:, 3 * head :])
            for k in range(chips):
                at = slice(k * rows, (k + 1) * rows)
                for i in range(4):
                    part = a[at, i * head : (i + 1) * head]
                    outs[k][n * 5 + i] = part.astype(BF)
                outs[k][n * 5 + 4] = b[at].astype(BF)

        def put(n, low, high, block):
            cols = slice(block * head, (block + 1) * head)
            gram = sum(dot(w[low][:, 3 * head :], w[high][:, cols], TN) for w in (ws, vs))
            for k in range(chips):
                for i in range(tall):
                    part = gram[i * rows : (i + 1) * rows]
                    outs[k][len(wanted) * 5 + n * tall + i] = part.astype(BF)

        for n, j in enumerate(wanted):
            if j == 0:
                put(n, 0, 0, 3)
                continue
            below = p < (p ^ j)
            at = first + n
            for core in range(CORES):
                pl.when(below & (c == core))(functools.partial(put, n, 0, at, core))
                pl.when(jnp.logical_not(below) & (c == core))(
                    functools.partial(put, n, at, 0, CORES + core)
                )

    return pl.pallas_call(
        kernel,
        name="project",
        out_shape=[jax.ShapeDtypeStruct((blocks, rows, head), BF)] * chips
        if apart
        else [jax.ShapeDtypeStruct((chips, blocks, rows, head), BF)],
        in_specs=vmem(1 + 2 * given),
        out_specs=vmem(chips if apart else 1),
        cost_estimate=cost(len(wanted) * 2**31, 4 * given * half * head * 8),
        compiler_params=pltpu.CompilerParams(vmem_limit_bytes=VMEM_BYTES),
    )(tokens, *own, *other)


def chain(rounds, squares, docs, head, width, seq):
    sections = sum(len(wanted) for wanted, _, _ in rounds)
    rows = squares.shape[0]
    lanes = sections * 4 * head
    flat = []
    for _, partials, grams in rounds:
        flat += [*partials] + [g for pair in grams for g in pair]

    def kernel(*refs):
        sq_ref, doc_ref = refs[:2]
        out, a_all, gram = refs[-3:]
        p, _, c = place()
        left = list(refs[2:-3])
        for wanted, partials, grams in rounds:
            a_refs = [left.pop(0) for _ in partials]
            for n, j in enumerate(wanted):
                for i in range(5):
                    at = n * 5 + i
                    if len(a_refs) > 1:
                        parts = [ref[at].astype(F32) for ref in a_refs]
                    else:
                        count = a_refs[0].shape[0]
                        parts = [a_refs[0][z, at].astype(F32) for z in range(count)]
                    a_all[p ^ j, i] = sum(parts)
            for i in range(sections):
                for h in range(CORES):
                    g_ref = left.pop(0)
                    for n, j in enumerate(wanted):
                        one, two = p ^ i, p ^ i ^ j
                        low, high = jnp.minimum(one, two), jnp.maximum(one, two)
                        if j > 0:
                            kind = jnp.where(one < two, 0, CORES) + (c ^ h)
                            gram[low, high, kind] = g_ref[n]
                        elif h == 0:
                            gram[low, high, 3] = g_ref[n]

        def times(m, low, high, kind, dims=NN):
            return dot(m, gram[low, high, kind], dims)

        places_r = lax.broadcasted_iota(jnp.int32, (rows, rows), 0)
        places_c = lax.broadcasted_iota(jnp.int32, (rows, rows), 1)
        across_docs = jnp.broadcast_to(doc_ref[p], (rows, rows))
        down = jnp.sum(jnp.where(places_r == places_c, across_docs, 0), axis=-1, keepdims=True)
        allowed = (places_r >= places_c) & (down == across_docs)
        if rows > seq:
            allowed = allowed & (places_r // seq == places_c // seq)
        scale = head ** (-0.5)

        x = [[a_all[s, i] for i in range(3)] for s in range(sections)]
        ho = [a_all[s, 3] for s in range(sections)]
        bo = [a_all[s, 4] for s in range(sections)]
        norm = sq_ref[...]
        saved = []
        for s in range(sections):
            inv = lax.rsqrt(jnp.maximum(norm, 0.0) / width + 1e-05)
            q, k, v = ((part * inv).astype(BF) for part in x[s])
            scores = jnp.where(allowed, dot(q, k, NT) * scale, -1e30)
            highest = jnp.max(scores, axis=-1, keepdims=True)
            exponent = jnp.where(allowed, jnp.exp(scores - highest), 0.0)
            soft = exponent / jnp.sum(exponent, axis=-1, keepdims=True)
            attend = soft.astype(BF)
            mixed = dot(attend, v).astype(BF)
            saved.append((inv, q, k, v, soft, attend, mixed, list(ho)))
            if s < sections - 1:
                before = ho[s]
                for t in range(s + 1, sections):
                    x[t] = [x[t][i] + times(mixed, s, t, i) for i in range(3)]
                for t in range(sections - 1):
                    if t >= s:
                        ho[t] = ho[t] + times(mixed, s, t, 3)
                    else:
                        ho[t] = ho[t] + times(mixed, t, s, 3, NT)
                wide = mixed.astype(F32)
                norm = norm + jnp.sum(wide * (before + ho[s]), axis=-1, keepdims=True)

        lane = lax.broadcasted_iota(jnp.int32, (rows, head), 1)
        scalars = jnp.zeros((rows, head), F32)
        for s in reversed(range(sections)):
            inv, q, k, v, soft, attend, mixed, along = saved[s]
            d_mixed = bo[s].astype(BF)
            d_attend = dot(d_mixed, v, NT).astype(BF).astype(F32)
            d_values = dot(attend, d_mixed, TN)
            inner = jnp.sum(soft * d_attend, axis=-1, keepdims=True)
            d_scores = (soft * (d_attend - inner) * scale).astype(BF)
            d_query = dot(d_scores, k)
            d_keys = dot(d_scores, q, TN)
            y = [(part * inv).astype(BF) for part in (d_query, d_keys, d_values)]
            inner = sum(y[i].astype(F32) * x[s][i] for i in range(3))
            coef = inv * inv * jnp.sum(inner, axis=-1, keepdims=True) / width
            for t in range(s):
                add = sum(times(y[i], t, s, i, NT) for i in range(3))
                bo[t] = bo[t] + add - coef * along[t]
            at = s * 4 * head
            for i in range(3):
                out[:, at + i * head : at + (i + 1) * head] = y[i]
            out[:, at + 3 * head : at + 4 * head] = mixed
            coarse = coef.astype(BF).astype(F32)
            scalars = jnp.where(lane == 2 * s, coarse, scalars)
            scalars = jnp.where(lane == 2 * s + 1, coef - coarse, scalars)
        out[:, lanes:] = scalars.astype(BF)

    return pl.pallas_call(
        kernel,
        name="chain",
        out_shape=jax.ShapeDtypeStruct((rows, lanes + head), BF),
        in_specs=vmem(2 + len(flat)),
        out_specs=pl.BlockSpec(memory_space=pltpu.VMEM),
        scratch_shapes=[
            pltpu.VMEM((sections, 5, rows, head), F32),
            pltpu.VMEM((sections, sections, 4, head, head), BF),
        ],
        cost_estimate=cost(sections * 2**31, 2**22),
        compiler_params=pltpu.CompilerParams(vmem_limit_bytes=VMEM_BYTES),
    )(squares, docs, *flat)


def rebuild(tokens, coefs, weights, halves, head, apart):
    groups, sections = len(coefs), len(weights[0])
    chips, rows, lanes = coefs[0].shape
    half = weights[0][0].shape[0]
    some = chips * rows
    count = groups * some
    block = min(1024 if len(halves) > 1 else 512, half)
    steps = half // block
    wide = len(halves) * half
    chosen = [weights[h] for h in halves]

    def kernel(*refs):
        t_refs, c_refs = refs[:groups], refs[groups : 2 * groups]
        w_refs = refs[2 * groups : 2 * groups + len(halves) * sections]
        outs = refs[2 * groups + len(halves) * sections : -7]
        h_out, g_out, left, edge, h_all, g_all, kept = refs[-7:]
        p, z, _ = place()
        outs = outs if apart else [outs[0].at[z ^ k] for k in range(chips)]
        out_w = slice(3 * head, 4 * head)
        qkv_w = slice(0, 3 * head)

        @pl.when(pl.program_id(0) == 0)
        def _():
            for i in range(groups):
                at = pl.ds(i * some, some)
                scalars = c_refs[i][:, :, lanes - head :].reshape(some, head).astype(F32)
                side = lax.broadcasted_iota(jnp.int32, scalars.shape, 1) // 2
                here = jnp.where(side == p, scalars, 0.0)
                here = jnp.sum(here, axis=-1, keepdims=True)
                edge[1, at, :] = jnp.broadcast_to(here, (some, head))
                for j in range(sections):
                    s = p ^ j
                    start = pl.multiple_of(s * 4 * head, 4 * head)
                    both = c_refs[i][:, :, pl.ds(start, 4 * head)].reshape(some, 4 * head)
                    left[j, at, :] = both
                    m = both[:, out_w]

                    def weigh(j=j, s=s, m=m):
                        later = jnp.where((side > s) & (side < sections), scalars, 0.0)
                        share = jnp.sum(later, axis=-1, keepdims=True)
                        left[j, at, out_w] = (-share * m.astype(F32)).astype(BF)
                        if j == 0:
                            edge[0, at, :] = jnp.broadcast_to(share, (some, head))

                    if j == 0:
                        weigh()
                    else:
                        pl.when(s > p)(weigh)

        for i in range(groups):
            for k in range(chips):
                at = pl.ds(i * some + k * rows, rows)
                h_all[at, :] = t_refs[i][z ^ k, 0].astype(F32)
                g_all[at, :] = t_refs[i][z ^ k, 1].astype(F32)

        def add(held):
            for j in range(1, sections):

                @pl.when((p ^ j) < p)
                def _():
                    h_all[...] += dot(left[j, :, out_w], held[j][:, out_w], NT)

                @pl.when((p ^ j) > p)
                def _():
                    g_all[...] += dot(left[j], held[j][...], NT)

            g_all[...] += dot(left[0, :, out_w], held[0][:, out_w], NT)
            kept[...] = dot(left[0, :, qkv_w], held[0][:, qkv_w], NT)

        for n in range(len(halves)):
            held = w_refs[n * sections : (n + 1) * sections]
            if len(halves) == 1:
                add(held)
            else:
                pl.when(pl.program_id(0) // steps == n)(functools.partial(add, held))

        h = h_all[...]
        g = g_all[...] - edge[0][:, :1] * h
        h_out[...] = h.astype(BF)
        g_out[...] = g.astype(BF)
        result = (g + kept[...] - edge[1][:, :1] * h).astype(BF)
        for i in range(groups):
            for k in range(chips):
                at = i * some + k * rows
                outs[k][i] = result[at : at + rows]

    if apart:
        shapes = [(groups, rows, wide)] * chips
        specs = [pl.BlockSpec((groups, rows, block), lambda i: (0, 0, i))] * chips
    else:
        shapes = [(chips, groups, rows, wide)]
        specs = [pl.BlockSpec((chips, groups, rows, block), lambda i: (0, 0, 0, i))]
    first = halves[0] * steps
    outs = pl.pallas_call(
        kernel,
        name="rebuild",
        grid=(wide // block,),
        out_shape=[jax.ShapeDtypeStruct(shape, BF) for shape in [*shapes] + [(count, wide)] * 2],
        in_specs=[pl.BlockSpec((chips, 2, rows, block), lambda i: (0, 0, 0, i + first))] * groups
        + vmem(groups)
        + [
            pl.BlockSpec(
                (block, 4 * head), lambda i, n=n: (jnp.clip(i - n * steps, 0, steps - 1), 0)
            )
            for n in range(len(halves))
            for _ in range(sections)
        ],
        out_specs=specs + [pl.BlockSpec((count, block), lambda i: (0, i))] * 2,
        scratch_shapes=[
            pltpu.VMEM((sections, count, 4 * head), BF),
            pltpu.VMEM((2, count, head), F32),
            pltpu.VMEM((count, block), F32),
            pltpu.VMEM((count, block), F32),
            pltpu.VMEM((count, block), F32),
        ],
        cost_estimate=cost(12 * count * wide * head * 4 * sections, 2**24),
        compiler_params=pltpu.CompilerParams(vmem_limit_bytes=VMEM_BYTES),
    )(*tokens, *coefs, *[w for held in chosen for w in held])
    return outs[:-2], outs[-2], outs[-1]


def gradients(built, coefs, order, half, h, head, dtype):
    chips, rows, lanes = coefs[0].shape
    some = chips * rows
    block = min(512, half)
    taken = [(hs, gs, halves.index(h)) for hs, gs, halves in built if h in halves]

    def kernel(*refs):
        n = len(taken)
        h_refs, g_refs, c_refs, out = refs[:n], refs[n : 2 * n], refs[2 * n : -1], refs[-1]
        start = pl.multiple_of(lax.axis_index("pipe") * 4 * head, 4 * head)
        own = [c_refs[i][:, :, pl.ds(start, 4 * head)].reshape(some, 4 * head) for i in order]
        own = jnp.concatenate(own, axis=0)
        hs = jnp.concatenate([ref[...] for ref in h_refs], axis=0)
        gs = jnp.concatenate([ref[...] for ref in g_refs], axis=0)
        out[:, : 3 * head] = dot(hs, own[:, : 3 * head], TN).astype(dtype)
        out[:, 3 * head :] = dot(gs, own[:, 3 * head :], TN).astype(dtype)

    specs = [
        pl.BlockSpec((hs.shape[0], block), lambda i, at=at: (0, i + at * (half // block)))
        for hs, _, at in taken
    ]
    return pl.pallas_call(
        kernel,
        name="gradients",
        grid=(half // block,),
        out_shape=jax.ShapeDtypeStruct((half, 4 * head), dtype),
        in_specs=specs * 2 + vmem(len(coefs)),
        out_specs=pl.BlockSpec((block, 4 * head), lambda i: (i, 0)),
        cost_estimate=cost(2**33, 2**23),
        compiler_params=pltpu.CompilerParams(vmem_limit_bytes=VMEM_BYTES),
    )(*[hs for hs, _, _ in taken], *[gs for _, gs, _ in taken], *coefs)


def rebuild_wide(tokens, coefs, weights, column, head):
    sections = len(weights)
    chips, rows, lanes = coefs[0].shape
    half = weights[0].shape[0]
    p, z, _ = place()
    grads = jnp.zeros((half, 4 * head), F32)
    results = []
    for both, coef in zip(tokens, coefs):
        both, coef, grads = lax.optimization_barrier((both, coef, grads))
        both = jnp.take(both[..., column : column + half], jnp.arange(chips) ^ z, axis=0)
        coef = coef.reshape(chips * rows, lanes)
        scalars = coef[:, lanes - head :].astype(F32)
        side = lax.broadcasted_iota(jnp.int32, scalars.shape, 1) // 2

        def share(s, scalars=scalars, side=side):
            after = jnp.where((side > s) & (side < sections), scalars, 0.0)
            return jnp.sum(after, axis=-1, keepdims=True)

        h = both[:, 0].reshape(chips * rows, half).astype(F32)
        g = both[:, 1].reshape(chips * rows, half).astype(F32)
        for j in range(sections):
            s = p ^ j
            part = lax.dynamic_slice_in_dim(coef, s * 4 * head, 4 * head, axis=1)
            y, m = part[:, : 3 * head], part[:, 3 * head :]
            out_w = weights[j][:, 3 * head :]
            if j == 0:
                own = part
            h = h + dot(jnp.where(s < p, m, jnp.zeros_like(m)), out_w, NT)
            g = g + dot(jnp.where(s > p, y, jnp.zeros_like(y)), weights[j][:, : 3 * head], NT)
            late = jnp.where(s >= p, -share(s) * m.astype(F32), 0.0).astype(BF)
            g = g + dot(late, out_w, NT)
        g = g - share(p) * h
        y, m = own[:, : 3 * head], own[:, 3 * head :]
        here = jnp.sum(jnp.where(side == p, scalars, 0.0), axis=-1, keepdims=True)
        grads = grads + jnp.concatenate(
            [dot(h.astype(BF), y, TN), dot(g.astype(BF), m, TN)], axis=1
        )
        result = (g + dot(y, weights[0][:, : 3 * head], NT) - here * h).astype(BF)
        results.append(result.reshape(chips, rows, half))
    result = jnp.stack(results, axis=1)
    return jnp.take(result, jnp.arange(chips) ^ z, axis=0), grads


def shards(inputs, segments, cotangent, w_query, w_key, w_value, w_out):
    sections = lax.axis_size("pipe")
    chips = lax.axis_size("dp") // CORES
    head = w_query.shape[2]
    _, batches, seq, width = inputs.shape
    short = -batches % sections
    if short:
        fill = ((0, 0), (0, short), (0, 0), (0, 0))
        inputs, cotangent = jnp.pad(inputs, fill), jnp.pad(cotangent, fill)
        segments = jnp.pad(segments, fill[:3])
    group = inputs.shape[1] // sections
    rows = group * seq

    pieces, squares = pack(inputs, cotangent, chips)
    mine = jnp.concatenate([w_query[0], w_key[0], w_value[0], w_out[0]], axis=1)
    pieces, mine = lax.optimization_barrier((pieces, mine))
    def summed(wanted, part):
        low = len(wanted) * 5
        if len(part) > 1:
            gram = sum(one[low:].astype(F32) for one in part)
        else:
            gram = jnp.sum(part[0][:, low:].astype(F32), axis=0)
        gram = gram.astype(BF).reshape(len(wanted), head, head)
        close = [gram] + [hop(gram, "pipe", j) for j in range(1, sections)]
        return wanted, part, [(g, hop(g, "dp", 1)) for g in close]

    tokens = across(pieces, chips)
    if sections == 4:
        near = hop(mine, "dp", 1)
        one, two = sides(mine)
        low, high = corner(one, two)
        near_one, near_two = (hop(w, "dp", 1) for w in after((one, two), tokens))
        ours, theirs = [mine, one, two], [near, near_one, near_two]
        early = project(tokens, ours, theirs, (0, 1, 2), head, False)
        low, high = after((low, high), *early)
        ours.append(jnp.concatenate([low, high], axis=0))
        theirs.append(hop(ours[3], "dp", 1))
        late = project(tokens, [mine, ours[3]], [near, theirs[3]], (3,), head, False)
        spread = sides(after(tokens, ours[3]))
        early = summed((0, 1, 2), [across(early[0], chips)])
        late = across(after(late[0], early[1]), chips)
        late = summed((3,), [after(late, early[2][0])])
        rounds = [early, late]
        plane = [pair[0] for pair in early[2]]
        spread = [tokens, *spread, jnp.concatenate(corner(*after(spread, plane)), axis=0)]
    else:
        ours = fan(mine)
        theirs = [hop(w, "dp", 1) for w in ours]
        spread = fan(tokens)
        wanted = tuple(range(sections))
        part = project(tokens, ours, theirs, wanted, head, False)
        rounds = [summed(wanted, [across(part[0], chips)])]

    docs = segments.reshape(sections, 1, rows)
    coef = chain(rounds, squares, docs, head, width, seq)
    coef = jnp.stack([coef] + [hop(coef, "dp", k * CORES) for k in range(1, chips)])

    half = mine.shape[0]
    if sections == 4:
        sent, built, raw = [], [], []

        def task(groups, halves, apart, before=(), between=()):
            token, scale = [spread[i] for i in groups], [coefs[i] for i in groups]
            token, scale = after((token, scale), *before)
            part, hs, gs = rebuild(token, scale, (ours, theirs), halves, head, apart)
            built.append((hs, gs, halves))
            raw.append(part)
            part = after(part, *between)
            if apart:
                part = [part[0]] + [hop(part[k], "dp", k * CORES) for k in range(1, chips)]
            else:
                part = [across(part[0], chips)]
            sent.append((part, groups, halves))

        coefs = [coef]
        task((0,), (0, 1), False)
        coefs += sides(after(coef, spread[3]))
        task((1, 2), (1,), True)
        task((1, 2), (0,), False, before=sent[0][0])
        coefs.append(jnp.concatenate(corner(*coefs[1:]), axis=0))
        task((3,), (0, 1), True, before=(sent[1][0], raw[2]), between=sent[1][0])
        halves_of = [halves for _, _, halves in built]
        token = hop(raw[3][0][:1, :8, :head], "dp", 1)
        arrays = after([pair[:2] for pair in built], sent[2][0], token)
        built = [(*pair, halves) for pair, halves in zip(arrays, halves_of)]
        far_grads = gradients(built, coefs, range(4), half, 1, head, BF)
        grads = gradients(built, coefs, range(4), half, 0, head, F32)
    else:
        coefs = fan(coef)
        far, far_grads = rebuild_wide(spread, coefs, theirs, half, head)
        close, grads = rebuild_wide(spread, coefs, ours, 0, head)
        order = tuple(range(sections))
        sent = [([across(far, chips)], order, (1,)), ([across(close, chips)], order, (0,))]
    far_grads = hop(far_grads, "dp", 1)
    grads = [
        (grads[:, at : at + head] + far_grads[:, at : at + head].astype(F32))[None]
        for at in range(0, 4 * head, head)
    ]
    arrays, grads = lax.optimization_barrier(([part for part, _, _ in sent], grads))
    sent = [(part, groups, halves) for part, (_, groups, halves) in zip(arrays, sent)]
    stored = unpack(sent, width)[: batches * seq]
    return (stored.reshape(1, 1, batches, seq, width), *grads)


def solution(mesh):
    wide = P("dp", None, None, None)
    weight = P("pipe", "dp", None)
    return jax.shard_map(
        shards,
        mesh=mesh,
        in_specs=(wide, P("dp", None, None), wide, weight, weight, weight, weight),
        out_specs=(P("pipe", "dp", None, None, None), weight, weight, weight, weight),
        check_vma=False,
    )
```
